128 devices in a mesh: dp: 8 (over x, core), cent: 16 (over z, y).
Axes of the slice: x: 4, y: 4, z: 4, core: 2. Of those that a mesh axis runs over, the one named last changes fastest.
Arguments:
- points: bfloat16 [131072, 1024], P(('dp', 'cent')), may hold values from -16 to 16
- point_cluster: int32 [131072], P(('dp', 'cent')), may hold values from 0 to 32767, as said below
- cand_blocks: int32 [1024, 8], P(('dp', 'cent')), may hold values from 0 to 31, as said below
- cent1_prev: float32 [32768, 1024], P(('dp', 'cent')), may hold values from -6 to 6
- parent: int32 [32768], P(('dp', 'cent')), may hold values from 0 to 4095, as said below
- cent2_prev: bfloat16 [4096, 1024], P('dp'), may hold values from -6 to 6
Outputs:
- cent1_new: float32 [32768, 1024], P(('dp', 'cent'))
- cent2_new: float32 [4096, 1024], P('dp')
- point_score: float32 [131072], P(('dp', 'cent'))
The draws below stay inside these ranges and needn't reach their ends.
Inputs may be any that keep to these rules, and one draw needn't show every extreme that they name: All points of an aligned block of 128 points share one level-one block (point_cluster // 128); on a device these block numbers never fall; the points of a device at index i of dp name only centroids from i * 16 * 256 to (i + 1) * 16 * 256 - 1; at most 2 point blocks of one device fall to one owner's 256 centroids, and in every draw one owner in each index of dp receives exactly 2 blocks from every device of that index. `parent`: the level-one centroids held at index i of dp name level-two centroids from i * 512 to (i + 1) * 512 - 1. `cand_blocks`: each row lists 8 different level-two blocks.
All inputs are finite; a program needn't handle non-finite values.
Results may differ from the reference program's by a relative error of at most 0.00094.
Values may be sent and summed in bfloat16 or wider, within the bound.
A program may use at most 128 MiB of HBM per device.

```python
import jax
import jax.numpy as jnp
from jax import lax

D = 1024
BLOCK = 128
PT_DEV = 1024
CAP = 2
C1_DEV = 256
C2_DEV = 512
NCAND = 8
C1 = 32768
N_DP = 8
N_CENT = 16


def shared_table(key):
    level_two = C2_DEV * N_DP
    table_key = jax.random.fold_in(key, 11)
    values = jnp.clip(jax.random.normal(table_key, (level_two, D), jnp.float32), -6.0, 6.0)
    return values


def shared_cands(key):
    block_rows = PT_DEV * N_DP * N_CENT // BLOCK
    upper_blocks = C2_DEV * N_DP // BLOCK
    scores = jax.random.randint(jax.random.fold_in(key, 13), (block_rows, upper_blocks), 0, 4096)
    scores = scores * upper_blocks + jnp.arange(upper_blocks, dtype=jnp.int32)[None, :]
    _, picked = lax.top_k(scores, NCAND)
    return picked.astype(jnp.int32)


def draw_cand_blocks(key, part):
    return shared_cands(key)


def draw_cent2_prev(key, part):
    return shared_table(key).astype(jnp.bfloat16)


def draw_points(key, part):
    total = PT_DEV * N_DP * N_CENT
    table = shared_table(key)
    cands = shared_cands(key)
    key_slot, key_row, key_mix, key_noise = jax.random.split(jax.random.fold_in(key, 17), 4)
    slot = jax.random.randint(key_slot, (total,), 0, NCAND)
    block_of = jnp.arange(total, dtype=jnp.int32) // BLOCK
    chosen_block = cands[block_of, slot]
    row = chosen_block * BLOCK + jax.random.randint(key_row, (total,), 0, BLOCK)
    anchor = table[row]
    mix = jax.random.uniform(key_mix, (total, 1), jnp.float32, 0.0, 0.65)
    noise = jnp.clip(jax.random.normal(key_noise, (total, D), jnp.float32), -6.0, 6.0)
    values = mix * anchor + jnp.sqrt(1.0 - mix * mix) * noise
    return values.astype(jnp.bfloat16)


def draw_point_cluster(key, part):
    device_total = N_DP * N_CENT
    block_total = PT_DEV // BLOCK
    slot_total = N_CENT * CAP
    owned_blocks = C1_DEV // BLOCK
    key_base, key_heat, key_forced, key_local, key_offset = jax.random.split(jax.random.fold_in(key, 71), 5)
    initial_score = jax.random.randint(key_base, (device_total, slot_total), 0, 4096)
    heat_rows = jax.random.randint(key_heat, (N_DP, N_CENT), 0, 4) * 4096
    heat_devices = jnp.repeat(heat_rows, N_CENT, axis=0)
    hotness_positions = jnp.repeat(heat_devices, CAP, axis=1)
    forced_rows = jax.random.randint(key_forced, (N_DP, 1), 0, N_CENT)
    pinned_workers = jnp.repeat(forced_rows, N_CENT, axis=0)
    position_index = jnp.arange(slot_total, dtype=jnp.int32)
    position_holder = position_index // CAP
    extra_reward = jnp.where(position_holder[None, :] == pinned_workers, 1 << 29, 0)
    precedence_rank = (initial_score + hotness_positions) * 4096 + position_index[None, :] + extra_reward
    _, chosen = lax.top_k(precedence_rank, block_total)
    local_block = jax.random.randint(key_local, (device_total, slot_total), 0, owned_blocks)
    chosen_local = jnp.take_along_axis(local_block, chosen, axis=1)
    chosen_owner = chosen // CAP
    composite = (chosen_owner * owned_blocks + chosen_local) * slot_total + chosen
    composite = jnp.sort(composite, axis=1)
    block_number = composite // slot_total
    row_index = jnp.arange(device_total, dtype=jnp.int32) // N_CENT
    first_ids = (row_index[:, None] * N_CENT * owned_blocks + block_number) * BLOCK
    offsets = jax.random.randint(key_offset, (device_total, block_total, BLOCK), 0, BLOCK)
    return (first_ids[:, :, None] + offsets).reshape(-1).astype(jnp.int32)


def draw_parent(key, part):
    level_one = C1_DEV * N_DP * N_CENT
    row_index = jnp.arange(level_one, dtype=jnp.int32) // (N_CENT * C1_DEV)
    offsets = jax.random.randint(jax.random.fold_in(key, 93), (level_one,), 0, C2_DEV)
    return (offsets + row_index * C2_DEV).astype(jnp.int32)


def shard_levels(rng, extent, shards, smallest, high):
    def one(axis_at, shards_of):
        draws = jax.random.uniform(jax.random.fold_in(jax.random.fold_in(rng, 6), axis_at), (shards_of,), jnp.float32, smallest / len(shards), high / len(shards))
        return jnp.repeat(jnp.exp(draws), extent[axis_at] // shards_of).reshape((-1,) + (1,) * (len(extent) - axis_at - 1))

    loudness = one(*shards[0])
    for cut in shards[1:]:
        loudness = loudness * one(*cut)
    return loudness


def gaussian(own_key, shape, scale, bound, cuts=(), kind=jnp.bfloat16):
    result = jax.random.normal(own_key, shape, jnp.float32) * scale
    if len(cuts) > 0:
        result = shard_levels(own_key, shape, cuts, -0.22, 0.18) * result
    return jnp.clip(result, min=-bound, max=bound).astype(kind)


def setup_inputs(seed: int = 0) -> dict:
    arg_keys = jax.random.split(jax.random.key(seed), 7)
    points = draw_points(jax.random.fold_in(arg_keys[6], 71), 0)
    point_cluster = draw_point_cluster(jax.random.fold_in(arg_keys[6], 71), 0)
    cand_blocks = draw_cand_blocks(jax.random.fold_in(arg_keys[6], 71), 0)
    cent1_prev = gaussian(arg_keys[3], (C1, D), 1.0, 6.0, ((0, 128),), jnp.float32)
    parent = draw_parent(jax.random.fold_in(arg_keys[6], 71), 0)
    cent2_prev = draw_cent2_prev(jax.random.fold_in(arg_keys[6], 71), 0)
    return {"points": points, "point_cluster": point_cluster, "cand_blocks": cand_blocks, "cent1_prev": cent1_prev, "parent": parent, "cent2_prev": cent2_prev}


EPSILON = 1e-06
SHARPNESS = 20.0

def rms_norm(values):
    return values * lax.rsqrt(lax.optimization_barrier(jnp.mean(values * values, axis=-1, keepdims=True)) + EPSILON)

def reference(points, point_cluster, cand_blocks, cent1_prev, parent, cent2_prev):
    devices_all = N_DP * N_CENT
    level_one = C1_DEV * devices_all
    level_two = C2_DEV * N_DP
    width = points.shape[1]
    point_groups = points.reshape(devices_all, PT_DEV, width)
    cluster_groups = point_cluster.reshape(devices_all, PT_DEV)

    def accumulate(carry, item):
        level_sums, counts = carry
        group_points, group_ids = item
        level_sums = level_sums + jax.ops.segment_sum(group_points.astype(jnp.float32), group_ids, num_segments=level_one)
        counts = counts + jax.ops.segment_sum(jnp.ones((PT_DEV,), jnp.float32), group_ids, num_segments=level_one)
        return ((level_sums, counts), None)
    start_state = (jnp.zeros((level_one, width), jnp.float32), jnp.zeros((level_one,), jnp.float32))
    (level_sums, counts), _ = lax.scan(accumulate, start_state, (point_groups, cluster_groups))
    average = level_sums / jnp.maximum(counts, 1.0)[:, None]
    cent1_new = rms_norm(average + cent1_prev)
    upper_sums = jax.ops.segment_sum(cent1_new, parent, num_segments=level_two)
    cent2_new = rms_norm(upper_sums)
    table = rms_norm(cent2_prev.astype(jnp.float32)).astype(jnp.bfloat16)
    table_blocks = table.reshape(level_two // BLOCK, BLOCK, width)
    unit_points = rms_norm(points.astype(jnp.float32)).astype(jnp.bfloat16)
    blocks_per = PT_DEV // BLOCK
    unit_groups = unit_points.reshape(devices_all, blocks_per, BLOCK, width)
    cand_groups = cand_blocks.reshape(devices_all, blocks_per, NCAND)

    def score_group(item):
        group_units, group_cands = item
        chosen = table_blocks[group_cands]
        products = jnp.einsum('bpd,bkcd->bpkc', group_units.astype(jnp.float32), chosen.astype(jnp.float32))
        weights = jnp.exp(products * (SHARPNESS / width))
        return jnp.log(lax.optimization_barrier(jnp.sum(weights, axis=(2, 3)))).reshape(PT_DEV)
    point_score = lax.map(score_group, (unit_groups, cand_groups)).reshape(-1)
    return (cent1_new, cent2_new, point_score)
```

```python
import jax
import jax.numpy as jnp
from jax import lax
from jax.experimental import pallas as pl
from jax.experimental.pallas import tpu as pltpu
from jax.sharding import PartitionSpec as P

BLOCK = 128
EPSILON = 1e-06
SHARPNESS = 20.0
RING = 4
MESH = pl.DeviceIdType.MESH
F32 = jnp.float32
BF16 = jnp.bfloat16


def rms_norm(values):
    return values * lax.rsqrt(jnp.mean(values * values, axis=-1, keepdims=True) + EPSILON)


def kernel(
    pts_hbm, ids_hbm, cand_ref, prev_hbm, parent_ref, tab_hbm,
    c1_ref, c2_ref, score_ref,
    pts, units, gathered, raw, table, mask, score_acc, ids_all, onehot, part, part_f, part_q, prev,
    up, up_f, up_q, low, low_f, low_q, send_sem, recv_sem, local_sem,
):
    dp = lax.axis_index("dp")
    cent = lax.axis_index("cent")
    x, core = dp // 2, lax.rem(dp, 2)
    z, y = cent // RING, lax.rem(cent, RING)

    def ring(at, step):
        return lax.rem(at + step + RING, RING)

    def y_at(step):
        return {"cent": z * RING + ring(y, step)}

    def z_at(step):
        return {"cent": ring(z, step) * RING + y}

    def x_at(step):
        return {"dp": ring(x, step) * 2 + core}

    partner = {"dp": x * 2 + 1 - core}
    copies = []

    def send(src, dst, device):
        at = len(copies)
        copy = pltpu.make_async_remote_copy(
            src_ref=src, dst_ref=dst, send_sem=send_sem.at[at], recv_sem=recv_sem.at[at],
            device_id=device, device_id_type=MESH,
        )
        copy.start()
        copies.append(copy)
        return copy

    fetches = [
        pltpu.make_async_copy(tab_hbm, raw, local_sem.at[0]),
        pltpu.make_async_copy(pts_hbm, pts, local_sem.at[1]),
        pltpu.make_async_copy(ids_hbm, ids_all.at[cent], local_sem.at[2]),
        pltpu.make_async_copy(prev_hbm, prev, local_sem.at[3]),
    ]
    for fetch in fetches:
        fetch.start()

    barrier = pltpu.get_barrier_semaphore()
    peers = [y_at(1), y_at(-1), y_at(2), z_at(1), z_at(-1), z_at(2), x_at(1), x_at(-1), partner]
    for peer in peers:
        pl.semaphore_signal(barrier, inc=1, device_id=peer, device_id_type=MESH)
    pl.semaphore_wait(barrier, len(peers))

    half = pts.shape[0] // 2
    wide = pts.shape[1] // 2
    lines = ((y_at, z_at), (z_at, y_at))

    first, last = pl.ds(0, half), pl.ds(half, half)
    moved = []
    for h in range(2):
        cols = pl.ds(h * wide, wide)
        near = lines[h][0]
        moved.append(dict(
            pa=send(pts_hbm.at[first, cols], gathered.at[h, 0, first], near(1)),
            mb=send(pts_hbm.at[last, cols], gathered.at[h, 1, last], near(-1)),
        ))
    id_copies = [send(ids_hbm, ids_all.at[cent], y_at(s)) for s in (1, -1, 2)]
    for h in range(2):
        cols = pl.ds(h * wide, wide)
        near = lines[h][0]
        moved[h].update(
            pb=send(pts_hbm.at[last, cols], gathered.at[h, 0, last], near(1)),
            ma=send(pts_hbm.at[first, cols], gathered.at[h, 1, first], near(-1)),
        )

    rows_t = raw.shape[0]
    top, bottom = pl.ds(0, rows_t // 2), pl.ds(rows_t // 2, rows_t // 2)
    fetches[0].wait()

    def norm_table(i, carry):
        rows = pl.ds(pl.multiple_of(i * 64, 64), 64)
        table[dp, rows] = rms_norm(raw[rows].astype(F32)).astype(BF16)
        return carry

    lax.fori_loop(0, rows_t // 64, norm_table, 0)
    own = table.at[dp]
    tab = dict(
        pa=send(own.at[top], own.at[top], x_at(1)),
        mb=send(own.at[bottom], own.at[bottom], x_at(-1)),
        pb=send(own.at[bottom], own.at[bottom], x_at(1)),
        ma=send(own.at[top], own.at[top], x_at(-1)),
        cp=send(own, own, partner),
    )

    for b in range(pts.shape[0] // BLOCK):
        rows = lax.broadcasted_iota(jnp.int32, (mask.shape[0], mask.shape[1], BLOCK), 0) * mask.shape[1]
        rows = rows + lax.broadcasted_iota(jnp.int32, (mask.shape[0], mask.shape[1], BLOCK), 1)
        hit = jnp.zeros(rows.shape, F32)
        for j in range(cand_ref.shape[1]):
            hit = jnp.where(rows == cand_ref[b, j], 1.0, hit)
        mask[:, :, b * BLOCK:(b + 1) * BLOCK] = hit
    score_acc[...] = jnp.zeros_like(score_acc)

    fetches[1].wait()

    def norm_points(i, carry):
        rows = pl.ds(pl.multiple_of(i * 64, 64), 64)
        units[rows] = rms_norm(pts[rows].astype(F32)).astype(BF16)
        return carry

    lax.fori_loop(0, pts.shape[0] // 64, norm_points, 0)

    def score(slot):
        def step(i, carry):
            at = pl.ds(pl.multiple_of(i * 256, 256), 256)
            dots = lax.dot_general(
                table[slot], units[at], (((1,), (1,)), ((), ())), preferred_element_type=F32
            )
            weights = jnp.exp(dots * (SHARPNESS / pts.shape[1]))
            sums = jnp.sum(weights.reshape(mask.shape[1], BLOCK, 256), axis=1)
            score_acc[:, at] += sums * mask[slot, :, at]
            return carry

        lax.fori_loop(0, pts.shape[0] // 256, step, 0)

    fetches[2].wait()
    for copy in id_copies:
        copy.wait_recv()
    rows_ids = ids_all.at[pl.ds(z * RING, RING)]
    id_copies = [send(rows_ids, rows_ids, z_at(s)) for s in (1, -1, 2)]

    own_rows = part.shape[2]
    group_base = dp * (RING * RING * own_rows)

    def owner_base(h, d):
        at = (ring(z, d) * RING + y) if h == 0 else (z * RING + ring(y, d))
        return group_base + at * own_rows

    def source_at(h, step):
        return (z * RING + ring(y, step)) if h == 0 else (ring(z, step) * RING + y)

    def accumulate(h, step, points, lo, dests, fresh=False):
        ids = ids_all[source_at(h, step), :, lo:lo + half]
        count = len(dests)
        for i, d in enumerate(dests):
            target = lax.broadcasted_iota(jnp.int32, (own_rows, half), 0) + owner_base(h, d)
            onehot[i * own_rows:(i + 1) * own_rows] = jnp.where(target == ids, 1.0, 0.0).astype(BF16)
        sums = jnp.dot(onehot[:count * own_rows], points, preferred_element_type=F32)
        for i, d in enumerate(dests):
            piece = sums[i * own_rows:(i + 1) * own_rows]
            if fresh:
                part[h, d] = piece
            else:
                part[h, d] += piece

    every = (0, 1, 2, 3)
    for h in range(2):
        cols = slice(h * wide, (h + 1) * wide)
        accumulate(h, 0, pts[0:half, cols], 0, every, fresh=True)
        accumulate(h, 0, pts[half:, cols], half, every)
    score(dp)
    for copy in id_copies:
        copy.wait_recv()

    for h in range(2):
        near = lines[h][0]
        moved[h]["pa"].wait_recv()
        moved[h]["fa"] = send(gathered.at[h, 0, first], gathered.at[h, 2, first], near(1))
        moved[h]["mb"].wait_recv()
        moved[h]["fb"] = send(gathered.at[h, 1, last], gathered.at[h, 2, last], near(-1))
    before = table.at[ring(x, -1) * 2 + core]
    after = table.at[ring(x, 1) * 2 + core]
    across = table.at[ring(x, 2) * 2 + core]
    tab["pa"].wait_recv()
    tab["fa"] = send(before.at[top], before.at[top], x_at(1))
    tab["mb"].wait_recv()
    tab["fb"] = send(after.at[bottom], after.at[bottom], x_at(-1))
    for h in range(2):
        accumulate(h, -1, gathered[h, 0, 0:half], 0, every)
        accumulate(h, 1, gathered[h, 1, half:], half, every)
    tab["cp"].wait_recv()
    other = 1 - core
    score(x * 2 + other)

    def count(i, carry):
        target = lax.broadcasted_iota(jnp.int32, (own_rows, BLOCK), 0) + (group_base + cent * own_rows)
        for j in range(ids_all.shape[2] // BLOCK):
            carry = carry + jnp.where(target == ids_all[i, :, j * BLOCK:(j + 1) * BLOCK], 1.0, 0.0)
        return carry

    counts = lax.fori_loop(0, ids_all.shape[0], count, jnp.zeros((own_rows, BLOCK), F32))
    counts = jnp.maximum(jnp.sum(counts, axis=1, keepdims=True), 1.0)

    for h in range(2):
        moved[h]["pb"].wait_recv()
        accumulate(h, -1, gathered[h, 0, half:], half, every)
        moved[h]["ma"].wait_recv()
        accumulate(h, 1, gathered[h, 1, 0:half], 0, every)
    tab["pb"].wait_recv()
    tab["q0"] = send(before, before, partner)
    tab["ma"].wait_recv()
    tab["q1"] = send(after, after, partner)
    score(ring(x, -1) * 2 + core)
    score(ring(x, 1) * 2 + core)
    tab["q0"].wait_recv()
    score(ring(x, -1) * 2 + other)
    tab["q1"].wait_recv()
    score(ring(x, 1) * 2 + other)

    class Scatter:
        def __init__(self, src, f, q, line):
            self.src, self.f, self.q, self.line = src, f, q, line
            self.n = q.shape[1] // 2

        def far(self):
            a, b = pl.ds(0, self.n), pl.ds(self.n, self.n)
            self.c2a = send(self.src(2).at[a], self.f.at[0], self.line(1))
            self.c2b = send(self.src(2).at[b], self.f.at[1], self.line(-1))

        def near(self):
            a, b = pl.ds(0, self.n), pl.ds(self.n, self.n)
            self.c1b = send(self.src(1).at[b], self.q.at[0, b], self.line(1))
            self.c3a = send(self.src(3).at[a], self.q.at[1, a], self.line(-1))

        def forward(self):
            a, b = pl.ds(0, self.n), pl.ds(self.n, self.n)
            self.c2a.wait_recv()
            self.src(1)[a] += self.f[0]
            self.c1a = send(self.src(1).at[a], self.q.at[0, a], self.line(1))
            self.c2b.wait_recv()
            self.src(3)[b] += self.f[1]
            self.c3b = send(self.src(3).at[b], self.q.at[1, b], self.line(-1))

        def wait(self):
            for copy in (self.c1b, self.c3a, self.c1a, self.c3b):
                copy.wait_recv()

    def scatter_part(h):
        return Scatter(lambda d: part.at[h, d], part_f.at[h], part_q.at[h], lines[h][1])

    sums = [scatter_part(h) for h in range(2)]
    for h in range(2):
        moved[h]["fa"].wait_recv()
        accumulate(h, 2, gathered[h, 2, 0:half], 0, (2,))
        moved[h]["fb"].wait_recv()
        accumulate(h, 2, gathered[h, 2, half:], half, (2,))
        sums[h].far()
    for h in range(2):
        accumulate(h, 2, gathered[h, 2, 0:half], 0, (1, 3))
        accumulate(h, 2, gathered[h, 2, half:], half, (1, 3))
        sums[h].near()
    for h in range(2):
        accumulate(h, 2, gathered[h, 2, 0:half], 0, (0,))
        accumulate(h, 2, gathered[h, 2, half:], half, (0,))
    tab["fa"].wait_recv()
    tab["fb"].wait_recv()
    tab["q2"] = send(across, across, partner)
    for h in range(2):
        sums[h].forward()
    score(ring(x, 2) * 2 + core)
    tab["q2"].wait_recv()
    score(ring(x, 2) * 2 + other)
    totals = jnp.sum(score_acc[...], axis=0, keepdims=True)
    for b in range(pts.shape[0] // BLOCK):
        score_ref[b:b + 1, :] = jnp.log(totals[:, b * BLOCK:(b + 1) * BLOCK])
    fetches[3].wait()
    for h in range(2):
        sums[h].wait()
    averages = [(part[h, 0] + part_q[h, 0] + part_q[h, 1]) / counts + prev[:, h * wide:(h + 1) * wide] for h in range(2)]
    squares = sum(jnp.sum(v * v, axis=1, keepdims=True) for v in averages)
    scale = lax.rsqrt(squares / pts.shape[1] + EPSILON)
    for h in range(2):
        c1_ref[:, h * wide:(h + 1) * wide] = averages[h] * scale

    block = up.shape[2]
    sub = block // RING
    local = parent_ref[...] - dp * (RING * block)
    swapped = (
        lax.shift_right_logical(local & (block - 1), 5) * block
        + lax.shift_right_logical(local, 7) * sub
        + (local & (sub - 1))
    )
    places = (local, swapped)
    me = ((z, y), (y, z))
    his, los = [], []
    for h in range(2):
        values = c1_ref[:, h * wide:(h + 1) * wide]
        hi = values.astype(BF16)
        his.append(hi)
        los.append((values - hi.astype(F32)).astype(BF16))

    def upper(h, d):
        target = lax.broadcasted_iota(jnp.int32, (block, own_rows), 0) + ring(me[h][0], d) * block
        pick = jnp.where(target == places[h], 1.0, 0.0).astype(BF16)
        up[h, d] = jnp.dot(pick, his[h], preferred_element_type=F32) + jnp.dot(
            pick, los[h], preferred_element_type=F32
        )

    def scatter_up(h):
        return Scatter(lambda d: up.at[h, d], up_f.at[h], up_q.at[h], lines[h][1])

    ups = [scatter_up(h) for h in range(2)]
    for h in range(2):
        upper(h, 2)
        ups[h].far()
    for h in range(2):
        upper(h, 1)
        upper(h, 3)
        ups[h].near()
    for h in range(2):
        upper(h, 0)
    for h in range(2):
        ups[h].forward()

    def scatter_low(h):
        return Scatter(lambda d: low.at[h, ring(me[h][1], d)], low_f.at[h], low_q.at[h], lines[h][0])

    lows = [scatter_low(h) for h in range(2)]
    for h in range(2):
        ups[h].wait()
        low[h] = (up[h, 0] + up_q[h, 0] + up_q[h, 1]).reshape(RING, sub, wide)
        lows[h].far()
        lows[h].near()
    for h in range(2):
        lows[h].forward()
    values = []
    for h in range(2):
        lows[h].wait()
        values.append(low[h, me[h][1]] + low_q[h, 0] + low_q[h, 1])
    squares = sum(jnp.sum(v * v, axis=1, keepdims=True) for v in values)
    scale = lax.rsqrt(squares / pts.shape[1] + EPSILON)
    for h in range(2):
        c2_ref[z, y, :, h * wide:(h + 1) * wide] = values[h] * scale

    class Gather:
        def __init__(self, place, at, line):
            self.place, self.at, self.line = place, at, line

        def start(self):
            at, place, line = self.at, self.place, self.line
            self.pa = send(place(at, 0), place(at, 0), line(1))
            self.mb = send(place(at, 1), place(at, 1), line(-1))
            self.pb = send(place(at, 1), place(at, 1), line(1))
            self.ma = send(place(at, 0), place(at, 0), line(-1))

        def forward(self):
            at, place, line = self.at, self.place, self.line
            self.pa.wait_recv()
            self.fa = send(place(ring(at, -1), 0), place(ring(at, -1), 0), line(1))
            self.mb.wait_recv()
            self.fb = send(place(ring(at, 1), 1), place(ring(at, 1), 1), line(-1))

        def wait(self):
            for copy in (self.pb, self.ma, self.fa, self.fb):
                copy.wait_recv()

    left, right = pl.ds(0, wide), pl.ds(wide, wide)
    small = [
        Gather(lambda k, s: c2_ref.at[z, k, pl.ds(s * (sub // 2), sub // 2), left], y, y_at),
        Gather(lambda k, s: c2_ref.at[k, y, pl.ds(s * (sub // 2), sub // 2), right], z, z_at),
    ]
    large = [
        Gather(lambda k, s: c2_ref.at[k, pl.ds(2 * s, 2), :, left], z, z_at),
        Gather(lambda k, s: c2_ref.at[pl.ds(2 * s, 2), k, :, right], y, y_at),
    ]
    for g in small:
        g.start()
    for g in small:
        g.forward()
    for g, l in zip(small, large):
        g.wait()
        l.start()
    for l in large:
        l.forward()
    for l in large:
        l.wait()
    for copy in copies:
        copy.wait_send()
    assert len(copies) == N_COPIES


N_COPIES = 88


def shards(points, point_cluster, cand_blocks, cent1_prev, parent, cent2_prev):
    rows, width = points.shape
    wide = width // 2
    owned = cent1_prev.shape[0]
    table_rows = cent2_prev.shape[0]
    n_dp = lax.axis_size("dp")
    n_cent = lax.axis_size("cent")
    block = table_rows // RING
    sub = block // RING
    any_spec = pl.BlockSpec(memory_space=pl.ANY)
    vmem = pl.BlockSpec(memory_space=pltpu.VMEM)
    smem = pl.BlockSpec(memory_space=pltpu.SMEM)
    cent1_new, cent2_new, score = pl.pallas_call(
        kernel,
        out_shape=(
            jax.ShapeDtypeStruct((owned, width), F32),
            jax.ShapeDtypeStruct((RING, RING, sub, width), F32),
            jax.ShapeDtypeStruct((rows // BLOCK, BLOCK), F32),
        ),
        in_specs=[any_spec, any_spec, smem, any_spec, vmem, any_spec],
        out_specs=(vmem, vmem, vmem),
        scratch_shapes=[
            pltpu.VMEM((rows, width), BF16),
            pltpu.VMEM((rows, width), BF16),
            pltpu.VMEM((2, 3, rows, wide), BF16),
            pltpu.VMEM((table_rows, width), BF16),
            pltpu.VMEM((n_dp, table_rows, width), BF16),
            pltpu.VMEM((n_dp, table_rows // BLOCK, rows), F32),
            pltpu.VMEM((table_rows // BLOCK, rows), F32),
            pltpu.VMEM((n_cent, 1, rows), jnp.int32),
            pltpu.VMEM((RING * owned, rows // 2), BF16),
            pltpu.VMEM((2, RING, owned, wide), F32),
            pltpu.VMEM((2, 2, owned // 2, wide), F32),
            pltpu.VMEM((2, 2, owned, wide), F32),
            pltpu.VMEM((owned, width), F32),
            pltpu.VMEM((2, RING, block, wide), F32),
            pltpu.VMEM((2, 2, block // 2, wide), F32),
            pltpu.VMEM((2, 2, block, wide), F32),
            pltpu.VMEM((2, RING, sub, wide), F32),
            pltpu.VMEM((2, 2, sub // 2, wide), F32),
            pltpu.VMEM((2, 2, sub, wide), F32),
            pltpu.SemaphoreType.DMA((N_COPIES,)),
            pltpu.SemaphoreType.DMA((N_COPIES,)),
            pltpu.SemaphoreType.DMA((4,)),
        ],
        compiler_params=pltpu.CompilerParams(
            collective_id=0, has_side_effects=True, vmem_limit_bytes=60 * 1024 * 1024
        ),
    )(
        points,
        point_cluster.reshape(1, rows),
        cand_blocks,
        cent1_prev,
        parent.reshape(1, owned),
        cent2_prev,
    )
    return cent1_new, cent2_new.reshape(table_rows, width), score.reshape(rows)


def solution(mesh):
    placed = (
        P(("dp", "cent"), None),
        P(("dp", "cent")),
        P(("dp", "cent"), None),
        P(("dp", "cent"), None),
        P(("dp", "cent")),
        P("dp", None),
    )
    return jax.shard_map(
        shards,
        mesh=mesh,
        in_specs=placed,
        out_specs=(P(("dp", "cent"), None), P("dp", None), P(("dp", "cent"))),
        check_vma=False,
    )
```

```python
import jax
import jax.numpy as jnp
from jax import lax
from jax.experimental import pallas as pl
from jax.experimental.pallas import tpu as pltpu
from jax.sharding import PartitionSpec as P

BLOCK = 128
EPSILON = 1e-06
SHARPNESS = 20.0
RING = 4
MESH = pl.DeviceIdType.MESH
F32 = jnp.float32
BF16 = jnp.bfloat16


def rms_norm(values):
    return values * lax.rsqrt(jnp.mean(values * values, axis=-1, keepdims=True) + EPSILON)


def kernel(
    pts_hbm, ids_hbm, cand_hbm, prev_hbm, parent_hbm, tab_hbm,
    c1_ref, c2_ref, score_ref,
    pts, units, gathered, raw, table, mask, score_acc, ids_all, onehot, across_hot, picks, part, part_f, part_q, prev,
    up, up_f, up_q, low, low_f, low_q, cand_ref, parent_ref, send_sem, recv_sem, local_sem,
):
    dp = lax.axis_index("dp")
    cent = lax.axis_index("cent")
    x, core = dp // 2, lax.rem(dp, 2)
    z, y = cent // RING, lax.rem(cent, RING)

    def ring(at, step):
        return lax.rem(at + step + RING, RING)

    def y_at(step):
        return {"cent": z * RING + ring(y, step)}

    def z_at(step):
        return {"cent": ring(z, step) * RING + y}

    def x_at(step):
        return {"dp": ring(x, step) * 2 + core}

    partner = {"dp": x * 2 + 1 - core}
    copies, pending = [], []

    def send(src, dst, device):
        at = len(copies)
        copy = pltpu.make_async_remote_copy(
            src_ref=src, dst_ref=dst, send_sem=send_sem.at[at], recv_sem=recv_sem.at[at],
            device_id=device, device_id_type=MESH,
        )
        copy.start()
        copies.append(copy)
        pending.append(copy)
        return copy

    def sent(copy):
        copy.wait_send()
        pending[:] = [other for other in pending if other is not copy]

    fetches = [
        pltpu.make_async_copy(tab_hbm, raw, local_sem.at[0]),
        pltpu.make_async_copy(pts_hbm, pts, local_sem.at[1]),
        pltpu.make_async_copy(ids_hbm, ids_all.at[cent], local_sem.at[2]),
        pltpu.make_async_copy(prev_hbm, prev, local_sem.at[3]),
        pltpu.make_async_copy(cand_hbm, cand_ref, local_sem.at[4]),
        pltpu.make_async_copy(parent_hbm, parent_ref, local_sem.at[5]),
    ]
    for fetch in fetches:
        fetch.start()

    barrier = pltpu.get_barrier_semaphore()
    peers = [y_at(1), y_at(-1), z_at(1), z_at(-1), x_at(1), x_at(-1), partner]
    for peer in peers:
        pl.semaphore_signal(barrier, inc=1, device_id=peer, device_id_type=MESH)
    pl.semaphore_wait(barrier, len(peers))

    half = pts.shape[0] // 2
    wide = pts.shape[1] // 2
    part_w = wide // 2
    lines = ((y_at, z_at), (z_at, y_at))

    first, last = pl.ds(0, half), pl.ds(half, half)
    moved = []
    for h in range(2):
        cols = pl.ds(h * wide, wide)
        near = lines[h][0]
        moved.append(dict(
            pa=send(pts_hbm.at[first, cols], gathered.at[h, 0, first], near(1)),
            mb=send(pts_hbm.at[last, cols], gathered.at[h, 1, last], near(-1)),
        ))
    id_near = [send(ids_hbm, ids_all.at[cent], y_at(1)), send(ids_hbm, ids_all.at[cent], y_at(-1))]

    rows_t = raw.shape[0]
    top, bottom = pl.ds(0, rows_t // 2), pl.ds(rows_t // 2, rows_t // 2)
    fetches[0].wait()

    def norm_table(i, carry):
        rows = pl.ds(pl.multiple_of(i * 64, 64), 64)
        table[dp, rows] = rms_norm(raw[rows].astype(F32)).astype(BF16)
        return carry

    lax.fori_loop(0, rows_t // 64, norm_table, 0)
    own = table.at[dp]
    tab = dict(
        pa=send(own.at[top], own.at[top], x_at(1)),
        mb=send(own.at[bottom], own.at[bottom], x_at(-1)),
        cp=send(own, own, partner),
    )

    fetches[4].wait()
    fetches[5].wait()
    for b in range(pts.shape[0] // BLOCK):
        rows = lax.broadcasted_iota(jnp.int32, (mask.shape[0], mask.shape[1], BLOCK), 0) * mask.shape[1]
        rows = rows + lax.broadcasted_iota(jnp.int32, (mask.shape[0], mask.shape[1], BLOCK), 1)
        hit = jnp.zeros(rows.shape, F32)
        for j in range(cand_ref.shape[1]):
            hit = jnp.where(rows == cand_ref[b, j], 1.0, hit)
        mask[:, :, b * BLOCK:(b + 1) * BLOCK] = hit
    score_acc[...] = jnp.zeros_like(score_acc)

    fetches[1].wait()

    def norm_points(i, carry):
        rows = pl.ds(pl.multiple_of(i * 64, 64), 64)
        units[rows] = rms_norm(pts[rows].astype(F32)).astype(BF16)
        return carry

    lax.fori_loop(0, pts.shape[0] // 64, norm_points, 0)

    for h in range(2):
        cols = pl.ds(h * wide, wide)
        near = lines[h][0]
        moved[h].update(
            pb=send(pts_hbm.at[last, cols], gathered.at[h, 0, last], near(1)),
            ma=send(pts_hbm.at[first, cols], gathered.at[h, 1, first], near(-1)),
        )
    tab.update(
        pb=send(own.at[bottom], own.at[bottom], x_at(1)),
        ma=send(own.at[top], own.at[top], x_at(-1)),
    )

    def score(slot):
        def step(i, carry):
            at = pl.ds(pl.multiple_of(i * 256, 256), 256)
            dots = lax.dot_general(
                table[slot], units[at], (((1,), (1,)), ((), ())), preferred_element_type=F32
            )
            weights = jnp.exp(dots * (SHARPNESS / pts.shape[1]))
            sums = jnp.sum(weights.reshape(mask.shape[1], BLOCK, 256), axis=1)
            score_acc[:, at] += sums * mask[slot, :, at]
            return carry

        lax.fori_loop(0, pts.shape[0] // 256, step, 0)

    fetches[2].wait()
    for copy in id_near:
        copy.wait_recv()
    passed_ids = ids_all.at[z * RING + ring(y, -1)]
    id_far = send(passed_ids, passed_ids, y_at(1))

    own_rows = part.shape[2]
    group_base = dp * (RING * RING * own_rows)

    def owner_base(h, d):
        at = (ring(z, d) * RING + y) if h == 0 else (z * RING + ring(y, d))
        return group_base + at * own_rows

    def source_at(h, step):
        return (z * RING + ring(y, step)) if h == 0 else (ring(z, step) * RING + y)

    def accumulate(h, step, points, lo, fresh=False):
        ids = ids_all[source_at(h, step), :, lo:lo + half]
        for d in range(RING):
            target = lax.broadcasted_iota(jnp.int32, (own_rows, half), 0) + owner_base(h, d)
            onehot[d * own_rows:(d + 1) * own_rows] = jnp.where(target == ids, 1.0, 0.0).astype(BF16)
        sums = jnp.dot(onehot[...], points, preferred_element_type=F32)
        for d in range(RING):
            for k in range(2):
                piece = sums[d * own_rows:(d + 1) * own_rows, k * part_w:(k + 1) * part_w]
                if fresh:
                    part[2 * k + h, d] = piece
                else:
                    part[2 * k + h, d] += piece

    def prepare(h):
        ids = ids_all[source_at(h, 2)]
        for d in range(RING):
            target = lax.broadcasted_iota(jnp.int32, (own_rows, 2 * half), 0) + owner_base(h, d)
            across_hot[h, d] = jnp.where(target == ids, 1.0, 0.0).astype(BF16)

    def finish(h, k, d):
        part[2 * k + h, d] += jnp.dot(
            across_hot[h, d], gathered[h, 2, :, k * part_w:(k + 1) * part_w], preferred_element_type=F32
        )

    cols = slice(0, wide), slice(wide, 2 * wide)
    accumulate(0, 0, pts[0:half, cols[0]], 0, fresh=True)
    accumulate(0, 0, pts[half:, cols[0]], half)
    id_far.wait_recv()
    rows_ids = ids_all.at[pl.ds(z * RING, RING)]
    id_near = [send(rows_ids, rows_ids, z_at(1)), send(rows_ids, rows_ids, z_at(-1))]
    score(dp)
    tab["cp"].wait_recv()
    other = 1 - core
    score(x * 2 + other)
    for copy in id_near:
        copy.wait_recv()
    passed_ids = ids_all.at[pl.ds(ring(z, -1) * RING, RING)]
    id_far = send(passed_ids, passed_ids, z_at(1))
    accumulate(1, 0, pts[0:half, cols[1]], 0, fresh=True)
    accumulate(1, 0, pts[half:, cols[1]], half)

    def pass_points(h, k):
        near = lines[h][0]
        cols = pl.ds(k * part_w, part_w)
        moved[h]["fa", k] = send(gathered.at[h, 0, first, cols], gathered.at[h, 2, first, cols], near(1))
        moved[h]["fb", k] = send(gathered.at[h, 1, last, cols], gathered.at[h, 2, last, cols], near(-1))

    for h in range(2):
        moved[h]["pa"].wait_recv()
        moved[h]["mb"].wait_recv()
        pass_points(h, 0)
    before = table.at[ring(x, -1) * 2 + core]
    after = table.at[ring(x, 1) * 2 + core]
    across = table.at[ring(x, 2) * 2 + core]
    for h in range(2):
        accumulate(h, -1, gathered[h, 0, 0:half], 0)
        accumulate(h, 1, gathered[h, 1, half:], half)
    for h in range(2):
        pass_points(h, 1)
    tab["pa"].wait_recv()
    tab["fa"] = send(before.at[top], before.at[top], x_at(1))
    tab["mb"].wait_recv()
    tab["fb"] = send(after.at[bottom], after.at[bottom], x_at(-1))
    id_far.wait_recv()

    def count(i, carry):
        target = lax.broadcasted_iota(jnp.int32, (own_rows, BLOCK), 0) + (group_base + cent * own_rows)
        for j in range(ids_all.shape[2] // BLOCK):
            carry = carry + jnp.where(target == ids_all[i, :, j * BLOCK:(j + 1) * BLOCK], 1.0, 0.0)
        return carry

    counts = lax.fori_loop(0, ids_all.shape[0], count, jnp.zeros((own_rows, BLOCK), F32))
    counts = jnp.maximum(jnp.sum(counts, axis=1, keepdims=True), 1.0)

    inverse = 1.0 / counts
    block = up.shape[2]
    sub = block // RING
    local = parent_ref[...] - dp * (RING * block)
    swapped = (
        lax.shift_right_logical(local & (block - 1), 5) * block
        + lax.shift_right_logical(local, 7) * sub
        + (local & (sub - 1))
    )
    places = (local, swapped)
    me = ((z, y), (y, z))
    for h in range(2):
        prepare(h)
        for d in range(RING):
            target = lax.broadcasted_iota(jnp.int32, (block, own_rows), 0) + ring(me[h][0], d) * block
            picks[h, d] = jnp.where(target == places[h], 1.0, 0.0).astype(BF16)

    for h in range(2):
        moved[h]["pb"].wait_recv()
        accumulate(h, -1, gathered[h, 0, half:], half)
        moved[h]["ma"].wait_recv()
        accumulate(h, 1, gathered[h, 1, 0:half], 0)
    tab["pb"].wait_recv()
    tab["q0"] = send(before, before, partner)
    tab["ma"].wait_recv()
    tab["q1"] = send(after, after, partner)

    class Scatter:
        def __init__(self, src, f, q, line):
            self.src, self.f, self.q, self.line = src, f, q, line
            self.n = q.shape[1] // 2

        def far(self):
            a, b = pl.ds(0, self.n), pl.ds(self.n, self.n)
            self.c2a = send(self.src(2).at[a], self.f.at[0], self.line(1))
            self.c2b = send(self.src(2).at[b], self.f.at[1], self.line(-1))

        def left(self):
            sent(self.c2a)
            sent(self.c2b)

        def near(self):
            a, b = pl.ds(0, self.n), pl.ds(self.n, self.n)
            self.c1b = send(self.src(1).at[b], self.q.at[0, b], self.line(1))
            self.c3a = send(self.src(3).at[a], self.q.at[1, a], self.line(-1))

        def forward(self):
            a, b = pl.ds(0, self.n), pl.ds(self.n, self.n)
            self.c2a.wait_recv()
            self.src(1)[a] += self.f[0]
            self.c1a = send(self.src(1).at[a], self.q.at[0, a], self.line(1))
            self.c2b.wait_recv()
            self.src(3)[b] += self.f[1]
            self.c3b = send(self.src(3).at[b], self.q.at[1, b], self.line(-1))

        def wait(self):
            for copy in (self.c1b, self.c3a, self.c1a, self.c3b):
                copy.wait_recv()

    def scatter(src, f, q, stage):
        return [Scatter(lambda d, g=g: src(g, d), f.at[g], q.at[g], lines[g % 2][stage]) for g in range(4)]

    def columns(g):
        at = (g % 2) * wide + (g // 2) * part_w
        return slice(at, at + part_w)

    sums = scatter(lambda g, d: part.at[g, d], part_f, part_q, 1)
    for k in range(2):
        for h in range(2):
            moved[h]["fa", k].wait_recv()
            moved[h]["fb", k].wait_recv()
            finish(h, k, 2)
            sums[2 * k + h].far()
        for h in range(2):
            finish(h, k, 1)
            finish(h, k, 3)
            if k == 0:
                sums[h].near()
        for h in range(2):
            finish(h, k, 0)
        score(ring(x, -1 + 2 * k) * 2 + core)
    sums[2].near()
    sums[3].near()
    sums[0].forward()
    sums[1].forward()
    tab["fa"].wait_recv()
    tab["fb"].wait_recv()
    tab["q2"] = send(across, across, partner)
    tab["q0"].wait_recv()
    score(ring(x, -1) * 2 + other)
    sums[2].forward()
    sums[3].forward()
    tab["q1"].wait_recv()
    score(ring(x, 1) * 2 + other)
    score(ring(x, 2) * 2 + core)
    tab["q2"].wait_recv()
    fetches[3].wait()
    squares = jnp.zeros((own_rows, 1), F32)
    for g in range(4):
        sums[g].wait()
        values = (part[g, 0] + part_q[g, 0] + part_q[g, 1]) * inverse + prev[:, columns(g)]
        c1_ref[:, columns(g)] = values
        squares = squares + jnp.sum(values * values, axis=1, keepdims=True)
    scale = lax.rsqrt(squares / pts.shape[1] + EPSILON)

    his, los = [], []
    for g in range(4):
        values = c1_ref[:, columns(g)] * scale
        c1_ref[:, columns(g)] = values
        hi = values.astype(BF16)
        his.append(hi)
        los.append((values - hi.astype(F32)).astype(BF16))

    def upper(g, d):
        pick = picks[g % 2, d]
        up[g, d] = jnp.dot(pick, his[g], preferred_element_type=F32) + jnp.dot(
            pick, los[g], preferred_element_type=F32
        )

    ups = scatter(lambda g, d: up.at[g, d], up_f, up_q, 1)
    for g in range(4):
        upper(g, 2)
        ups[g].far()
    for g in range(4):
        upper(g, 1)
        upper(g, 3)
    for g in range(4):
        ups[g].left()
        ups[g].near()
    for g in range(4):
        upper(g, 0)
    for g in range(4):
        ups[g].forward()
    score(ring(x, 2) * 2 + other)
    totals = jnp.sum(score_acc[...], axis=0, keepdims=True)
    for b in range(pts.shape[0] // BLOCK):
        score_ref[b:b + 1, :] = jnp.log(totals[:, b * BLOCK:(b + 1) * BLOCK])
    lows = scatter(lambda g, d: low.at[g, ring(me[g % 2][1], d)], low_f, low_q, 0)
    for g in range(4):
        ups[g].wait()
        low[g] = (up[g, 0] + up_q[g, 0] + up_q[g, 1]).reshape(RING, sub, part_w)
        lows[g].far()
        lows[g].near()
    for g in range(4):
        lows[g].forward()
    squares = jnp.zeros((sub, 1), F32)
    values = []
    for g in range(4):
        lows[g].wait()
        values.append(low[g, me[g % 2][1]] + low_q[g, 0] + low_q[g, 1])
        squares = squares + jnp.sum(values[g] * values[g], axis=1, keepdims=True)
    scale = lax.rsqrt(squares / pts.shape[1] + EPSILON)
    for g in range(4):
        c2_ref[z, y, :, columns(g)] = values[g] * scale

    def piece(h, i, j, rows=pl.ds(0, sub)):
        at = (i, j) if h == 0 else (j, i)
        return c2_ref.at[at[0], at[1], rows, pl.ds(h * wide, wide)]

    upper_half, lower_half = pl.ds(0, sub // 2), pl.ds(sub // 2, sub // 2)

    def spread(h, i, j, line):
        src = piece(h, i, j)
        return send(src, src, line(1)), send(src, src, line(-1))

    def pass_on(pair, low_src, high_src, line):
        pair[0].wait_recv()
        first_copy = send(low_src, low_src, line(1))
        pair[1].wait_recv()
        return first_copy, send(high_src, high_src, line(-1))

    def pass_far(h, j, pair):
        i = me[h][0]
        return pass_on(
            pair, piece(h, ring(i, -1), j, upper_half), piece(h, ring(i, 1), j, lower_half), lines[h][1]
        )

    near_pairs, far_pairs, passed = [], [], []
    for h in range(2):
        i, j = me[h]
        near_pairs.append(spread(h, i, j, lines[h][0]))
    for h in range(2):
        for copy in near_pairs[h]:
            sent(copy)
    for h in range(2):
        i, j = me[h]
        far_pairs.append({0: spread(h, i, j, lines[h][1])})
    crossed = []
    for h in range(2):
        i, j = me[h]
        crossed.append(pass_on(
            near_pairs[h], piece(h, i, ring(j, -1), upper_half), piece(h, i, ring(j, 1), lower_half), lines[h][0]
        ))
    for h in range(2):
        i, j = me[h]
        far_pairs[h][-1] = spread(h, i, ring(j, -1), lines[h][1])
        far_pairs[h][1] = spread(h, i, ring(j, 1), lines[h][1])
    for h in range(2):
        passed.append(pass_far(h, me[h][1], far_pairs[h][0]))
    for h in range(2):
        i, j = me[h]
        for copy in crossed[h]:
            copy.wait_recv()
        far_pairs[h][2] = spread(h, i, ring(j, 2), lines[h][1])
    for step in (-1, 1, 2):
        for h in range(2):
            passed.append(pass_far(h, ring(me[h][1], step), far_pairs[h][step]))
    for pair in passed:
        for copy in pair:
            copy.wait_recv()
    for copy in pending:
        copy.wait_send()
    assert len(copies) == N_COPIES


N_COPIES = 144


def shards(points, point_cluster, cand_blocks, cent1_prev, parent, cent2_prev):
    rows, width = points.shape
    wide = width // 2
    owned = cent1_prev.shape[0]
    table_rows = cent2_prev.shape[0]
    n_dp = lax.axis_size("dp")
    n_cent = lax.axis_size("cent")
    block = table_rows // RING
    sub = block // RING
    hbm = pl.BlockSpec(memory_space=pltpu.HBM)
    vmem = pl.BlockSpec(memory_space=pltpu.VMEM)
    cent1_new, cent2_new, score = pl.pallas_call(
        kernel,
        out_shape=(
            jax.ShapeDtypeStruct((owned, width), F32),
            jax.ShapeDtypeStruct((RING, RING, sub, width), F32),
            jax.ShapeDtypeStruct((rows // BLOCK, BLOCK), F32),
        ),
        in_specs=[hbm] * 6,
        out_specs=(vmem, vmem, vmem),
        scratch_shapes=[
            pltpu.VMEM((rows, width), BF16),
            pltpu.VMEM((rows, width), BF16),
            pltpu.VMEM((2, 3, rows, wide), BF16),
            pltpu.VMEM((table_rows, width), BF16),
            pltpu.VMEM((n_dp, table_rows, width), BF16),
            pltpu.VMEM((n_dp, table_rows // BLOCK, rows), F32),
            pltpu.VMEM((table_rows // BLOCK, rows), F32),
            pltpu.VMEM((n_cent, 1, rows), jnp.int32),
            pltpu.VMEM((RING * owned, rows // 2), BF16),
            pltpu.VMEM((2, RING, owned, rows), BF16),
            pltpu.VMEM((2, RING, block, owned), BF16),
            pltpu.VMEM((4, RING, owned, wide // 2), F32),
            pltpu.VMEM((4, 2, owned // 2, wide // 2), F32),
            pltpu.VMEM((4, 2, owned, wide // 2), F32),
            pltpu.VMEM((owned, width), F32),
            pltpu.VMEM((4, RING, block, wide // 2), F32),
            pltpu.VMEM((4, 2, block // 2, wide // 2), F32),
            pltpu.VMEM((4, 2, block, wide // 2), F32),
            pltpu.VMEM((4, RING, sub, wide // 2), F32),
            pltpu.VMEM((4, 2, sub // 2, wide // 2), F32),
            pltpu.VMEM((4, 2, sub, wide // 2), F32),
            pltpu.SMEM(cand_blocks.shape, jnp.int32),
            pltpu.VMEM((1, owned), jnp.int32),
            pltpu.SemaphoreType.DMA((N_COPIES,)),
            pltpu.SemaphoreType.DMA((N_COPIES,)),
            pltpu.SemaphoreType.DMA((6,)),
        ],
        compiler_params=pltpu.CompilerParams(
            collective_id=0, has_side_effects=True, vmem_limit_bytes=44 * 1024 * 1024
        ),
    )(
        pltpu.with_memory_space_constraint(points, pltpu.HBM),
        pltpu.with_memory_space_constraint(point_cluster.reshape(1, rows), pltpu.HBM),
        pltpu.with_memory_space_constraint(cand_blocks, pltpu.HBM),
        pltpu.with_memory_space_constraint(cent1_prev, pltpu.HBM),
        pltpu.with_memory_space_constraint(parent.reshape(1, owned), pltpu.HBM),
        pltpu.with_memory_space_constraint(cent2_prev, pltpu.HBM),
    )
    return cent1_new, cent2_new.reshape(table_rows, width), score.reshape(rows)


def solution(mesh):
    placed = (
        P(("dp", "cent"), None),
        P(("dp", "cent")),
        P(("dp", "cent"), None),
        P(("dp", "cent"), None),
        P(("dp", "cent")),
        P("dp", None),
    )
    return jax.shard_map(
        shards,
        mesh=mesh,
        in_specs=placed,
        out_specs=(P(("dp", "cent"), None), P("dp", None), P(("dp", "cent"))),
        check_vma=False,
    )
```

```python
import jax
import jax.numpy as jnp
from jax import lax
from jax.experimental import pallas as pl
from jax.experimental.pallas import tpu as pltpu
from jax.sharding import PartitionSpec as P

BLOCK = 128
EPSILON = 1e-06
SHARPNESS = 20.0
RING = 4
MESH = pl.DeviceIdType.MESH
F32 = jnp.float32
BF16 = jnp.bfloat16


def rms_norm(values):
    return values * lax.rsqrt(jnp.mean(values * values, axis=-1, keepdims=True) + EPSILON)


def kernel(
    pts_hbm, ids_hbm, cand_hbm, prev_hbm, parent_hbm, tab_hbm,
    c1_ref, c2_ref, score_ref,
    pts, units, gathered, raw, table, mask, score_acc, ids_all, onehot, across_hot, picks, part, part_f, part_q, prev,
    up, up_f, up_q, low, low_f, low_q, column_ids, cand_ref, parent_ref, send_sem, recv_sem, local_sem,
):
    dp = lax.axis_index("dp")
    cent = lax.axis_index("cent")
    x, core = dp // 2, lax.rem(dp, 2)
    z, y = cent // RING, lax.rem(cent, RING)

    def ring(at, step):
        return lax.rem(at + step + RING, RING)

    def y_at(step):
        return {"cent": z * RING + ring(y, step)}

    def z_at(step):
        return {"cent": ring(z, step) * RING + y}

    def x_at(step):
        return {"dp": ring(x, step) * 2 + core}

    partner = {"dp": x * 2 + 1 - core}
    copies = []

    def send(src, dst, device):
        at = len(copies)
        copy = pltpu.make_async_remote_copy(
            src_ref=src, dst_ref=dst, send_sem=send_sem.at[at], recv_sem=recv_sem.at[at],
            device_id=device, device_id_type=MESH,
        )
        copy.start()
        copies.append(copy)
        return copy

    fetches = [
        pltpu.make_async_copy(tab_hbm, raw, local_sem.at[0]),
        pltpu.make_async_copy(pts_hbm, pts, local_sem.at[1]),
        pltpu.make_async_copy(ids_hbm, ids_all.at[cent], local_sem.at[2]),
        pltpu.make_async_copy(prev_hbm, prev, local_sem.at[3]),
        pltpu.make_async_copy(cand_hbm, cand_ref, local_sem.at[4]),
        pltpu.make_async_copy(parent_hbm, parent_ref, local_sem.at[5]),
    ]
    for fetch in fetches:
        fetch.start()

    barrier = pltpu.get_barrier_semaphore()
    peers = [y_at(1), y_at(-1), z_at(1), z_at(-1), x_at(1), x_at(-1), partner]
    for peer in peers:
        pl.semaphore_signal(barrier, inc=1, device_id=peer, device_id_type=MESH)
    pl.semaphore_wait(barrier, len(peers))

    half = pts.shape[0] // 2
    wide = pts.shape[1] // 2
    part_w = wide // 2
    lines = ((y_at, z_at), (z_at, y_at))

    row_near = [send(ids_hbm, ids_all.at[cent], y_at(1)), send(ids_hbm, ids_all.at[cent], y_at(-1))]
    column_near = [send(ids_hbm, column_ids.at[0], z_at(1)), send(ids_hbm, column_ids.at[1], z_at(-1))]

    first, last = pl.ds(0, half), pl.ds(half, half)
    moved = []
    for h in range(2):
        cols = pl.ds(h * wide, wide)
        near = lines[h][0]
        moved.append(dict(
            pa=send(pts_hbm.at[first, cols], gathered.at[h, 0, first], near(1)),
            mb=send(pts_hbm.at[last, cols], gathered.at[h, 1, last], near(-1)),
        ))
    rows_t = raw.shape[0]
    top, bottom = pl.ds(0, rows_t // 2), pl.ds(rows_t // 2, rows_t // 2)
    fetches[0].wait()

    def norm_table(i, carry):
        rows = pl.ds(pl.multiple_of(i * 64, 64), 64)
        table[dp, rows] = rms_norm(raw[rows].astype(F32)).astype(BF16)
        return carry

    lax.fori_loop(0, rows_t // 64, norm_table, 0)
    own = table.at[dp]
    tab = dict(
        pa=send(own.at[top], own.at[top], x_at(1)),
        mb=send(own.at[bottom], own.at[bottom], x_at(-1)),
        cp=send(own, own, partner),
    )

    for copy in row_near + column_near:
        copy.wait_recv()
    passed_ids = ids_all.at[z * RING + ring(y, -1)]
    row_far = send(passed_ids, passed_ids, y_at(1))
    column_far = send(column_ids.at[0], column_ids.at[2], z_at(1))

    for h in range(2):
        cols = pl.ds(h * wide, wide)
        near = lines[h][0]
        moved[h].update(
            pb=send(pts_hbm.at[last, cols], gathered.at[h, 0, last], near(1)),
            ma=send(pts_hbm.at[first, cols], gathered.at[h, 1, first], near(-1)),
        )
    tab.update(
        pb=send(own.at[bottom], own.at[bottom], x_at(1)),
        ma=send(own.at[top], own.at[top], x_at(-1)),
    )

    fetches[4].wait()
    fetches[5].wait()
    for b in range(pts.shape[0] // BLOCK):
        rows = lax.broadcasted_iota(jnp.int32, (mask.shape[0], mask.shape[1], BLOCK), 0) * mask.shape[1]
        rows = rows + lax.broadcasted_iota(jnp.int32, (mask.shape[0], mask.shape[1], BLOCK), 1)
        hit = jnp.zeros(rows.shape, F32)
        for j in range(cand_ref.shape[1]):
            hit = jnp.where(rows == cand_ref[b, j], 1.0, hit)
        mask[:, :, b * BLOCK:(b + 1) * BLOCK] = hit
    score_acc[...] = jnp.zeros_like(score_acc)

    fetches[1].wait()

    def norm_points(i, carry):
        rows = pl.ds(pl.multiple_of(i * 64, 64), 64)
        units[rows] = rms_norm(pts[rows].astype(F32)).astype(BF16)
        return carry

    lax.fori_loop(0, pts.shape[0] // 64, norm_points, 0)

    def score(slot):
        def step(i, carry):
            at = pl.ds(pl.multiple_of(i * 256, 256), 256)
            dots = lax.dot_general(
                table[slot], units[at], (((1,), (1,)), ((), ())), preferred_element_type=F32
            )
            weights = jnp.exp(dots * (SHARPNESS / pts.shape[1]))
            sums = jnp.sum(weights.reshape(mask.shape[1], BLOCK, 256), axis=1)
            score_acc[:, at] += sums * mask[slot, :, at]
            return carry

        lax.fori_loop(0, pts.shape[0] // 256, step, 0)

    own_rows = part.shape[2]
    group_base = dp * (RING * RING * own_rows)

    def owner_base(h, d):
        at = (ring(z, d) * RING + y) if h == 0 else (z * RING + ring(y, d))
        return group_base + at * own_rows

    def ids_of(h, step):
        if h == 0 or step == 0:
            return ids_all.at[z * RING + ring(y, step)]
        return column_ids.at[{-1: 0, 1: 1, 2: 2}[step]]

    def accumulate(h, step, points, lo, fresh=False):
        ids = ids_of(h, step)[:, lo:lo + half]
        for d in range(RING):
            target = lax.broadcasted_iota(jnp.int32, (own_rows, half), 0) + owner_base(h, d)
            onehot[d * own_rows:(d + 1) * own_rows] = jnp.where(target == ids, 1.0, 0.0).astype(BF16)
        sums = jnp.dot(onehot[...], points, preferred_element_type=F32)
        for d in range(RING):
            for k in range(2):
                piece = sums[d * own_rows:(d + 1) * own_rows, k * part_w:(k + 1) * part_w]
                if fresh:
                    part[2 * k + h, d] = piece
                else:
                    part[2 * k + h, d] += piece

    def prepare(h):
        ids = ids_of(h, 2)[...]
        for d in range(RING):
            target = lax.broadcasted_iota(jnp.int32, (own_rows, 2 * half), 0) + owner_base(h, d)
            across_hot[h, d] = jnp.where(target == ids, 1.0, 0.0).astype(BF16)

    def finish(h, k, d):
        part[2 * k + h, d] += jnp.dot(
            across_hot[h, d], gathered[h, 2, :, k * part_w:(k + 1) * part_w], preferred_element_type=F32
        )

    fetches[2].wait()
    for h in range(2):
        cols = slice(h * wide, (h + 1) * wide)
        accumulate(h, 0, pts[0:half, cols], 0, fresh=True)
        accumulate(h, 0, pts[half:, cols], half)
    score(dp)

    def pass_points(h, k):
        near = lines[h][0]
        cols = pl.ds(k * part_w, part_w)
        moved[h]["fa", k] = send(gathered.at[h, 0, first, cols], gathered.at[h, 2, first, cols], near(1))
        moved[h]["fb", k] = send(gathered.at[h, 1, last, cols], gathered.at[h, 2, last, cols], near(-1))

    row_far.wait_recv()
    rows_ids = ids_all.at[pl.ds(z * RING, RING)]
    rows_near = [send(rows_ids, rows_ids, z_at(1)), send(rows_ids, rows_ids, z_at(-1))]
    for h in range(2):
        moved[h]["pa"].wait_recv()
        moved[h]["mb"].wait_recv()
        for k in range(2):
            pass_points(h, k)
    before = table.at[ring(x, -1) * 2 + core]
    after = table.at[ring(x, 1) * 2 + core]
    across = table.at[ring(x, 2) * 2 + core]
    tab["pa"].wait_recv()
    tab["fa"] = send(before.at[top], before.at[top], x_at(1))
    tab["mb"].wait_recv()
    tab["fb"] = send(after.at[bottom], after.at[bottom], x_at(-1))
    column_far.wait_recv()
    for h in range(2):
        accumulate(h, -1, gathered[h, 0, 0:half], 0)
        accumulate(h, 1, gathered[h, 1, half:], half)

    tab["cp"].wait_recv()
    other = 1 - core
    score(x * 2 + other)
    sub = up.shape[3]
    block = sub * RING
    local = parent_ref[...] - dp * (RING * block)
    swapped = (
        lax.shift_right_logical(local & (block - 1), 5) * block
        + lax.shift_right_logical(local, 7) * sub
        + (local & (sub - 1))
    )
    places = (local, swapped)
    me = ((z, y), (y, z))
    for h in range(2):
        prepare(h)
        for d in range(RING):
            target = lax.broadcasted_iota(jnp.int32, (block, own_rows), 0) + ring(me[h][0], d) * block
            picks[h, d] = jnp.where(target == places[h], 1.0, 0.0).astype(BF16)

    for h in range(2):
        moved[h]["pb"].wait_recv()
        accumulate(h, -1, gathered[h, 0, half:], half)
        moved[h]["ma"].wait_recv()
        accumulate(h, 1, gathered[h, 1, 0:half], 0)
    tab["pb"].wait_recv()
    tab["q0"] = send(before, before, partner)
    tab["ma"].wait_recv()
    tab["q1"] = send(after, after, partner)

    for copy in rows_near:
        copy.wait_recv()
    passed_ids = ids_all.at[pl.ds(ring(z, -1) * RING, RING)]
    rows_far = send(passed_ids, passed_ids, z_at(1))

    class Scatter:
        def __init__(self, src, f, q, line):
            self.src, self.f, self.q, self.line = src, f, q, line
            self.n = q.shape[1] // 2

        def far(self):
            a, b = pl.ds(0, self.n), pl.ds(self.n, self.n)
            self.c2a = send(self.src(2).at[a], self.f.at[0], self.line(1))
            self.c2b = send(self.src(2).at[b], self.f.at[1], self.line(-1))

        def near(self):
            a, b = pl.ds(0, self.n), pl.ds(self.n, self.n)
            self.c1b = send(self.src(1).at[b], self.q.at[0, b], self.line(1))
            self.c3a = send(self.src(3).at[a], self.q.at[1, a], self.line(-1))

        def forward(self):
            a, b = pl.ds(0, self.n), pl.ds(self.n, self.n)
            self.c2a.wait_recv()
            self.src(1)[a] += self.f[0]
            self.c1a = send(self.src(1).at[a], self.q.at[0, a], self.line(1))
            self.c2b.wait_recv()
            self.src(3)[b] += self.f[1]
            self.c3b = send(self.src(3).at[b], self.q.at[1, b], self.line(-1))

        def wait(self):
            for copy in (self.c1b, self.c3a, self.c1a, self.c3b):
                copy.wait_recv()

    def scatter(src, f, q, stage):
        return [Scatter(lambda d, g=g: src(g, d), f.at[g], q.at[g], lines[g % 2][stage]) for g in range(4)]

    def columns(g):
        at = (g % 2) * wide + (g // 2) * part_w
        return slice(at, at + part_w)

    sums = scatter(lambda g, d: part.at[g, d], part_f, part_q, 1)
    for k in range(2):
        for h in range(2):
            moved[h]["fa", k].wait_recv()
            moved[h]["fb", k].wait_recv()
            finish(h, k, 2)
            sums[2 * k + h].far()
        for h in range(2):
            finish(h, k, 1)
            finish(h, k, 3)
            sums[2 * k + h].near()
        for h in range(2):
            finish(h, k, 0)
        score(ring(x, -1 + 2 * k) * 2 + core)
    sums[0].forward()
    sums[1].forward()
    tab["fa"].wait_recv()
    tab["fb"].wait_recv()
    tab["q2"] = send(across, across, partner)
    sums[2].forward()
    sums[3].forward()
    rows_far.wait_recv()
    def count(i, carry):
        target = lax.broadcasted_iota(jnp.int32, (own_rows, BLOCK), 0) + (group_base + cent * own_rows)
        for j in range(ids_all.shape[2] // BLOCK):
            carry = carry + jnp.where(target == ids_all[i, :, j * BLOCK:(j + 1) * BLOCK], 1.0, 0.0)
        return carry

    counts = lax.fori_loop(0, ids_all.shape[0], count, jnp.zeros((own_rows, BLOCK), F32))
    counts = jnp.maximum(jnp.sum(counts, axis=1, keepdims=True), 1.0)

    inverse = 1.0 / counts
    fetches[3].wait()
    squares = jnp.zeros((own_rows, 1), F32)
    for g in range(4):
        sums[g].wait()
        values = (part[g, 0] + part_q[g, 0] + part_q[g, 1]) * inverse + prev[:, columns(g)]
        c1_ref[:, columns(g)] = values
        squares = squares + jnp.sum(values * values, axis=1, keepdims=True)
    scale = lax.rsqrt(squares / pts.shape[1] + EPSILON)

    his, los = [], []
    for h in range(2):
        values = c1_ref[:, h * wide:(h + 1) * wide] * scale
        c1_ref[:, h * wide:(h + 1) * wide] = values
        hi = values.astype(BF16)
        his.append(hi)
        los.append((values - hi.astype(F32)).astype(BF16))

    def upper(h, d):
        pick = picks[h, d]
        sums = jnp.dot(pick, his[h], preferred_element_type=F32) + jnp.dot(
            pick, los[h], preferred_element_type=F32
        )
        up[h, d] = sums.reshape(RING, sub, wide)

    def scatter_up(h, step):
        j = ring(me[h][1], step)
        return Scatter(lambda d: up.at[h, d, j], up_f.at[h, step], up_q.at[h, step], lines[h][1])

    def settle(h, step):
        ups[h][step].wait()
        j = ring(me[h][1], step)
        low[h, j] = up[h, 0, j] + up_q[h, step, 0] + up_q[h, step, 1]

    ups = [[scatter_up(h, step) for step in range(RING)] for h in range(2)]
    lows = [
        Scatter(lambda d, h=h: low.at[h, ring(me[h][1], d)], low_f.at[h], low_q.at[h], lines[h][0]) for h in range(2)
    ]
    for h in range(2):
        upper(h, 2)
        for step in (2, 1, 3, 0):
            ups[h][step].far()
    for h in range(2):
        upper(h, 1)
        upper(h, 3)
        ups[h][2].near()
    for h in range(2):
        upper(h, 0)
    for h in range(2):
        ups[h][2].forward()
    for h in range(2):
        for step in (1, 3):
            ups[h][step].near()
    for h in range(2):
        for step in (1, 3):
            ups[h][step].forward()
    for h in range(2):
        ups[h][0].near()
        ups[h][0].forward()
    tab["q0"].wait_recv()
    score(ring(x, -1) * 2 + other)
    for h in range(2):
        settle(h, 2)
        lows[h].far()
    for h in range(2):
        settle(h, 1)
        settle(h, 3)
        lows[h].near()
    for h in range(2):
        lows[h].forward()
    tab["q1"].wait_recv()
    score(ring(x, 1) * 2 + other)
    for h in range(2):
        settle(h, 0)
    squares = jnp.zeros((sub, 1), F32)
    values = []
    for h in range(2):
        lows[h].wait()
        values.append(low[h, me[h][1]] + low_q[h, 0] + low_q[h, 1])
        squares = squares + jnp.sum(values[h] * values[h], axis=1, keepdims=True)
    scale = lax.rsqrt(squares / pts.shape[1] + EPSILON)
    for h in range(2):
        c2_ref[z, y, :, h * wide:(h + 1) * wide] = values[h] * scale

    def piece(h, i, j, rows=pl.ds(0, sub)):
        at = (i, j) if h == 0 else (j, i)
        return c2_ref.at[at[0], at[1], rows, pl.ds(h * wide, wide)]

    upper_half, lower_half = pl.ds(0, sub // 2), pl.ds(sub // 2, sub // 2)

    def spread(h, i, j, line):
        src = piece(h, i, j)
        return send(src, src, line(1)), send(src, src, line(-1))

    def spread_halves(h, i, j, line):
        high, low_rows = piece(h, i, j, upper_half), piece(h, i, j, lower_half)
        first_pair = send(high, high, line(1)), send(low_rows, low_rows, line(-1))
        return first_pair + (send(low_rows, low_rows, line(1)), send(high, high, line(-1)))

    def pass_on(pair, low_src, high_src, line):
        pair[0].wait_recv()
        first_copy = send(low_src, low_src, line(1))
        pair[1].wait_recv()
        return first_copy, send(high_src, high_src, line(-1))

    def pass_far(h, j, pair):
        i = me[h][0]
        return pass_on(
            pair, piece(h, ring(i, -1), j, upper_half), piece(h, ring(i, 1), j, lower_half), lines[h][1]
        )

    near_pairs, far_pairs, passed = [], [], []
    for h in range(2):
        i, j = me[h]
        near_pairs.append(spread_halves(h, i, j, lines[h][0]))
    for h in range(2):
        i, j = me[h]
        far_pairs.append({0: spread(h, i, j, lines[h][1])})
    score(ring(x, 2) * 2 + core)
    crossed = []
    for h in range(2):
        i, j = me[h]
        crossed.append(pass_on(
            near_pairs[h], piece(h, i, ring(j, -1), upper_half), piece(h, i, ring(j, 1), lower_half), lines[h][0]
        ))
    for h in range(2):
        i, j = me[h]
        near_pairs[h][2].wait_recv()
        far_pairs[h][-1] = spread(h, i, ring(j, -1), lines[h][1])
        near_pairs[h][3].wait_recv()
        far_pairs[h][1] = spread(h, i, ring(j, 1), lines[h][1])
    for h in range(2):
        passed.append(pass_far(h, me[h][1], far_pairs[h][0]))
    tab["q2"].wait_recv()
    score(ring(x, 2) * 2 + other)
    for h in range(2):
        i, j = me[h]
        for copy in crossed[h]:
            copy.wait_recv()
        far_pairs[h][2] = spread_halves(h, i, ring(j, 2), lines[h][1])
    for step in (-1, 1, 2):
        for h in range(2):
            passed.append(pass_far(h, ring(me[h][1], step), far_pairs[h][step]))
    for h in range(2):
        passed.append(far_pairs[h][2][2:])
    totals = jnp.sum(score_acc[...], axis=0, keepdims=True)
    for b in range(pts.shape[0] // BLOCK):
        score_ref[b:b + 1, :] = jnp.log(totals[:, b * BLOCK:(b + 1) * BLOCK])
    for pair in passed:
        for copy in pair:
            copy.wait_recv()
    for copy in copies:
        copy.wait_send()
    assert len(copies) == N_COPIES


N_COPIES = 167


def shards(points, point_cluster, cand_blocks, cent1_prev, parent, cent2_prev):
    rows, width = points.shape
    wide = width // 2
    owned = cent1_prev.shape[0]
    table_rows = cent2_prev.shape[0]
    n_dp = lax.axis_size("dp")
    n_cent = lax.axis_size("cent")
    block = table_rows // RING
    sub = block // RING
    hbm = pl.BlockSpec(memory_space=pltpu.HBM)
    vmem = pl.BlockSpec(memory_space=pltpu.VMEM)
    cent1_new, cent2_new, score = pl.pallas_call(
        kernel,
        out_shape=(
            jax.ShapeDtypeStruct((owned, width), F32),
            jax.ShapeDtypeStruct((RING, RING, sub, width), F32),
            jax.ShapeDtypeStruct((rows // BLOCK, BLOCK), F32),
        ),
        in_specs=[hbm] * 6,
        out_specs=(vmem, vmem, vmem),
        scratch_shapes=[
            pltpu.VMEM((rows, width), BF16),
            pltpu.VMEM((rows, width), BF16),
            pltpu.VMEM((2, 3, rows, wide), BF16),
            pltpu.VMEM((table_rows, width), BF16),
            pltpu.VMEM((n_dp, table_rows, width), BF16),
            pltpu.VMEM((n_dp, table_rows // BLOCK, rows), F32),
            pltpu.VMEM((table_rows // BLOCK, rows), F32),
            pltpu.VMEM((n_cent, 1, rows), jnp.int32),
            pltpu.VMEM((RING * owned, rows // 2), BF16),
            pltpu.VMEM((2, RING, owned, rows), BF16),
            pltpu.VMEM((2, RING, block, owned), BF16),
            pltpu.VMEM((4, RING, owned, wide // 2), F32),
            pltpu.VMEM((4, 2, owned // 2, wide // 2), F32),
            pltpu.VMEM((4, 2, owned, wide // 2), F32),
            pltpu.VMEM((owned, width), F32),
            pltpu.VMEM((2, RING, RING, sub, wide), F32),
            pltpu.VMEM((2, RING, 2, sub // 2, wide), F32),
            pltpu.VMEM((2, RING, 2, sub, wide), F32),
            pltpu.VMEM((2, RING, sub, wide), F32),
            pltpu.VMEM((2, 2, sub // 2, wide), F32),
            pltpu.VMEM((2, 2, sub, wide), F32),
            pltpu.VMEM((3, 1, rows), jnp.int32),
            pltpu.SMEM(cand_blocks.shape, jnp.int32),
            pltpu.VMEM((1, owned), jnp.int32),
            pltpu.SemaphoreType.DMA((N_COPIES,)),
            pltpu.SemaphoreType.DMA((N_COPIES,)),
            pltpu.SemaphoreType.DMA((6,)),
        ],
        compiler_params=pltpu.CompilerParams(
            collective_id=0, has_side_effects=True, vmem_limit_bytes=44 * 1024 * 1024
        ),
    )(
        pltpu.with_memory_space_constraint(points, pltpu.HBM),
        pltpu.with_memory_space_constraint(point_cluster.reshape(1, rows), pltpu.HBM),
        pltpu.with_memory_space_constraint(cand_blocks, pltpu.HBM),
        pltpu.with_memory_space_constraint(cent1_prev, pltpu.HBM),
        pltpu.with_memory_space_constraint(parent.reshape(1, owned), pltpu.HBM),
        pltpu.with_memory_space_constraint(cent2_prev, pltpu.HBM),
    )
    return cent1_new, cent2_new.reshape(table_rows, width), score.reshape(rows)


def solution(mesh):
    placed = (
        P(("dp", "cent"), None),
        P(("dp", "cent")),
        P(("dp", "cent"), None),
        P(("dp", "cent"), None),
        P(("dp", "cent")),
        P("dp", None),
    )
    return jax.shard_map(
        shards,
        mesh=mesh,
        in_specs=placed,
        out_specs=(P(("dp", "cent"), None), P("dp", None), P(("dp", "cent"))),
        check_vma=False,
    )
```

```python
import jax
import jax.numpy as jnp
from jax import lax
from jax.experimental import pallas as pl
from jax.experimental.pallas import tpu as pltpu
from jax.sharding import PartitionSpec as P

BLOCK = 128
EPSILON = 1e-06
SHARPNESS = 20.0
RING = 4
MESH = pl.DeviceIdType.MESH
F32 = jnp.float32
BF16 = jnp.bfloat16


def rms_norm(values):
    return values * lax.rsqrt(jnp.mean(values * values, axis=-1, keepdims=True) + EPSILON)


def kernel(
    pts_hbm, ids_hbm, cand_hbm, prev_hbm, parent_hbm, tab_hbm,
    c1_ref, c2_ref, score_ref,
    pts, units, gathered, raw, table, mask, score_acc, ids_all, onehot, across_hot, picks, part, part_f, part_q, prev,
    up, up_f, up_q, low, low_f, low_q, column_ids, cand_ref, parent_ref, send_sem, recv_sem, local_sem,
):
    dp = lax.axis_index("dp")
    cent = lax.axis_index("cent")
    x, core = dp // 2, lax.rem(dp, 2)
    z, y = cent // RING, lax.rem(cent, RING)

    def ring(at, step):
        return lax.rem(at + step + RING, RING)

    def y_at(step):
        return {"cent": z * RING + ring(y, step)}

    def z_at(step):
        return {"cent": ring(z, step) * RING + y}

    def x_at(step):
        return {"dp": ring(x, step) * 2 + core}

    partner = {"dp": x * 2 + 1 - core}
    copies = []

    def send(src, dst, device):
        at = len(copies)
        copy = pltpu.make_async_remote_copy(
            src_ref=src, dst_ref=dst, send_sem=send_sem.at[at], recv_sem=recv_sem.at[at],
            device_id=device, device_id_type=MESH,
        )
        copy.start()
        copies.append(copy)
        return copy

    fetches = [
        pltpu.make_async_copy(tab_hbm, raw, local_sem.at[0]),
        pltpu.make_async_copy(pts_hbm, pts, local_sem.at[1]),
        pltpu.make_async_copy(ids_hbm, ids_all.at[cent], local_sem.at[2]),
        pltpu.make_async_copy(prev_hbm, prev, local_sem.at[3]),
        pltpu.make_async_copy(cand_hbm, cand_ref, local_sem.at[4]),
        pltpu.make_async_copy(parent_hbm, parent_ref, local_sem.at[5]),
    ]
    for fetch in fetches:
        fetch.start()

    barrier = pltpu.get_barrier_semaphore()
    peers = [y_at(1), y_at(-1), z_at(1), z_at(-1), x_at(1), x_at(-1), partner]
    for peer in peers:
        pl.semaphore_signal(barrier, inc=1, device_id=peer, device_id_type=MESH)
    pl.semaphore_wait(barrier, len(peers))

    half = pts.shape[0] // 2
    wide = pts.shape[1] // 2
    part_w = wide // 2
    lines = ((y_at, z_at), (z_at, y_at))

    row_near = [send(ids_hbm, ids_all.at[cent], y_at(1)), send(ids_hbm, ids_all.at[cent], y_at(-1))]
    column_near = [send(ids_hbm, column_ids.at[0], z_at(1)), send(ids_hbm, column_ids.at[1], z_at(-1))]

    first, last = pl.ds(0, half), pl.ds(half, half)
    moved = []
    for h in range(2):
        cols = pl.ds(h * wide, wide)
        near = lines[h][0]
        moved.append(dict(
            pa=send(pts_hbm.at[first, cols], gathered.at[h, 0, first], near(1)),
            mb=send(pts_hbm.at[last, cols], gathered.at[h, 1, last], near(-1)),
        ))
    rows_t = raw.shape[0]
    top, bottom = pl.ds(0, rows_t // 2), pl.ds(rows_t // 2, rows_t // 2)
    fetches[0].wait()

    def norm_table(i, carry):
        rows = pl.ds(pl.multiple_of(i * 64, 64), 64)
        table[dp, rows] = rms_norm(raw[rows].astype(F32)).astype(BF16)
        return carry

    lax.fori_loop(0, rows_t // 64, norm_table, 0)
    own = table.at[dp]
    tab = dict(
        pa=send(own.at[top], own.at[top], x_at(1)),
        mb=send(own.at[bottom], own.at[bottom], x_at(-1)),
        cp=send(own, own, partner),
    )

    for copy in row_near + column_near:
        copy.wait_recv()
    passed_ids = ids_all.at[z * RING + ring(y, -1)]
    row_far = send(passed_ids, passed_ids, y_at(1))
    column_far = send(column_ids.at[0], column_ids.at[2], z_at(1))

    for h in range(2):
        cols = pl.ds(h * wide, wide)
        near = lines[h][0]
        moved[h].update(
            pb=send(pts_hbm.at[last, cols], gathered.at[h, 0, last], near(1)),
            ma=send(pts_hbm.at[first, cols], gathered.at[h, 1, first], near(-1)),
        )
    tab.update(
        pb=send(own.at[bottom], own.at[bottom], x_at(1)),
        ma=send(own.at[top], own.at[top], x_at(-1)),
    )

    fetches[4].wait()
    fetches[5].wait()
    for b in range(pts.shape[0] // BLOCK):
        rows = lax.broadcasted_iota(jnp.int32, (mask.shape[0], mask.shape[1], BLOCK), 0) * mask.shape[1]
        rows = rows + lax.broadcasted_iota(jnp.int32, (mask.shape[0], mask.shape[1], BLOCK), 1)
        hit = jnp.zeros(rows.shape, F32)
        for j in range(cand_ref.shape[1]):
            hit = jnp.where(rows == cand_ref[b, j], 1.0, hit)
        mask[:, :, b * BLOCK:(b + 1) * BLOCK] = hit
    score_acc[...] = jnp.zeros_like(score_acc)

    fetches[1].wait()

    def norm_points(i, carry):
        rows = pl.ds(pl.multiple_of(i * 64, 64), 64)
        units[rows] = rms_norm(pts[rows].astype(F32)).astype(BF16)
        return carry

    lax.fori_loop(0, pts.shape[0] // 64, norm_points, 0)

    def score(slot):
        def step(i, carry):
            at = pl.ds(pl.multiple_of(i * 256, 256), 256)
            dots = lax.dot_general(
                table[slot], units[at], (((1,), (1,)), ((), ())), preferred_element_type=F32
            )
            weights = jnp.exp(dots * (SHARPNESS / pts.shape[1]))
            sums = jnp.sum(weights.reshape(mask.shape[1], BLOCK, 256), axis=1)
            score_acc[:, at] += sums * mask[slot, :, at]
            return carry

        lax.fori_loop(0, pts.shape[0] // 256, step, 0)

    own_rows = part.shape[2]
    group_base = dp * (RING * RING * own_rows)

    def owner_base(h, d):
        at = (ring(z, d) * RING + y) if h == 0 else (z * RING + ring(y, d))
        return group_base + at * own_rows

    def ids_of(h, step):
        if h == 0 or step == 0:
            return ids_all.at[z * RING + ring(y, step)]
        return column_ids.at[{-1: 0, 1: 1, 2: 2}[step]]

    def accumulate(h, step, points, lo, fresh=False):
        ids = ids_of(h, step)[:, lo:lo + half]
        for d in range(RING):
            target = lax.broadcasted_iota(jnp.int32, (own_rows, half), 0) + owner_base(h, d)
            onehot[d * own_rows:(d + 1) * own_rows] = jnp.where(target == ids, 1.0, 0.0).astype(BF16)
        sums = jnp.dot(onehot[...], points, preferred_element_type=F32)
        for d in range(RING):
            for k in range(2):
                piece = sums[d * own_rows:(d + 1) * own_rows, k * part_w:(k + 1) * part_w]
                if fresh:
                    part[2 * k + h, d] = piece
                else:
                    part[2 * k + h, d] += piece

    def prepare(h):
        ids = ids_of(h, 2)[...]
        for d in range(RING):
            target = lax.broadcasted_iota(jnp.int32, (own_rows, 2 * half), 0) + owner_base(h, d)
            across_hot[h, d] = jnp.where(target == ids, 1.0, 0.0).astype(BF16)

    def finish(h, k, d):
        part[2 * k + h, d] += jnp.dot(
            across_hot[h, d], gathered[h, 2, :, k * part_w:(k + 1) * part_w], preferred_element_type=F32
        )

    fetches[2].wait()
    for h in range(2):
        cols = slice(h * wide, (h + 1) * wide)
        accumulate(h, 0, pts[0:half, cols], 0, fresh=True)
        accumulate(h, 0, pts[half:, cols], half)
    score(dp)

    def pass_points(h, k):
        near = lines[h][0]
        cols = pl.ds(k * part_w, part_w)
        moved[h]["fa", k] = send(gathered.at[h, 0, first, cols], gathered.at[h, 2, first, cols], near(1))
        moved[h]["fb", k] = send(gathered.at[h, 1, last, cols], gathered.at[h, 2, last, cols], near(-1))

    row_far.wait_recv()
    rows_ids = ids_all.at[pl.ds(z * RING, RING)]
    rows_near = [send(rows_ids, rows_ids, z_at(1)), send(rows_ids, rows_ids, z_at(-1))]
    for h in range(2):
        moved[h]["pa"].wait_recv()
        moved[h]["mb"].wait_recv()
        for k in range(2):
            pass_points(h, k)
    before = table.at[ring(x, -1) * 2 + core]
    after = table.at[ring(x, 1) * 2 + core]
    across = table.at[ring(x, 2) * 2 + core]
    tab["pa"].wait_recv()
    tab["fa"] = send(before.at[top], before.at[top], x_at(1))
    tab["mb"].wait_recv()
    tab["fb"] = send(after.at[bottom], after.at[bottom], x_at(-1))
    column_far.wait_recv()
    for h in range(2):
        accumulate(h, -1, gathered[h, 0, 0:half], 0)
        accumulate(h, 1, gathered[h, 1, half:], half)

    tab["cp"].wait_recv()
    other = 1 - core
    score(x * 2 + other)
    sub = up.shape[3]
    block = sub * RING
    local = parent_ref[...] - dp * (RING * block)
    swapped = (
        lax.shift_right_logical(local & (block - 1), 5) * block
        + lax.shift_right_logical(local, 7) * sub
        + (local & (sub - 1))
    )
    places = (local, swapped)
    me = ((z, y), (y, z))
    for h in range(2):
        prepare(h)
        for d in range(RING):
            target = lax.broadcasted_iota(jnp.int32, (block, own_rows), 0) + ring(me[h][0], d) * block
            picks[h, d] = jnp.where(target == places[h], 1.0, 0.0).astype(BF16)

    for h in range(2):
        moved[h]["pb"].wait_recv()
        accumulate(h, -1, gathered[h, 0, half:], half)
        moved[h]["ma"].wait_recv()
        accumulate(h, 1, gathered[h, 1, 0:half], 0)
    tab["pb"].wait_recv()
    tab["q0"] = send(before, before, partner)
    tab["ma"].wait_recv()
    tab["q1"] = send(after, after, partner)

    for copy in rows_near:
        copy.wait_recv()
    passed_ids = ids_all.at[pl.ds(ring(z, -1) * RING, RING)]
    rows_far = send(passed_ids, passed_ids, z_at(1))

    class Scatter:
        def __init__(self, src, f, q, line):
            self.src, self.f, self.q, self.line = src, f, q, line
            self.n = q.shape[1] // 2

        def far(self):
            a, b = pl.ds(0, self.n), pl.ds(self.n, self.n)
            self.c2a = send(self.src(2).at[a], self.f.at[0], self.line(1))
            self.c2b = send(self.src(2).at[b], self.f.at[1], self.line(-1))

        def near(self):
            a, b = pl.ds(0, self.n), pl.ds(self.n, self.n)
            self.c1b = send(self.src(1).at[b], self.q.at[0, b], self.line(1))
            self.c3a = send(self.src(3).at[a], self.q.at[1, a], self.line(-1))

        def forward(self):
            a, b = pl.ds(0, self.n), pl.ds(self.n, self.n)
            self.c2a.wait_recv()
            self.src(1)[a] += self.f[0]
            self.c1a = send(self.src(1).at[a], self.q.at[0, a], self.line(1))
            self.c2b.wait_recv()
            self.src(3)[b] += self.f[1]
            self.c3b = send(self.src(3).at[b], self.q.at[1, b], self.line(-1))

        def wait(self):
            for copy in (self.c1b, self.c3a, self.c1a, self.c3b):
                copy.wait_recv()

    def scatter(src, f, q, stage):
        return [Scatter(lambda d, g=g: src(g, d), f.at[g], q.at[g], lines[g % 2][stage]) for g in range(4)]

    def columns(g):
        at = (g % 2) * wide + (g // 2) * part_w
        return slice(at, at + part_w)

    sums = scatter(lambda g, d: part.at[g, d], part_f, part_q, 1)
    for k in range(2):
        for h in range(2):
            moved[h]["fa", k].wait_recv()
            moved[h]["fb", k].wait_recv()
            finish(h, k, 2)
            sums[2 * k + h].far()
        for h in range(2):
            finish(h, k, 1)
            finish(h, k, 3)
            sums[2 * k + h].near()
        for h in range(2):
            finish(h, k, 0)
        score(ring(x, -1 + 2 * k) * 2 + core)
    sums[0].forward()
    sums[1].forward()
    tab["fa"].wait_recv()
    tab["fb"].wait_recv()
    tab["q2"] = send(across, across, partner)
    sums[2].forward()
    sums[3].forward()
    tab["q0"].wait_recv()
    score(ring(x, -1) * 2 + other)
    rows_far.wait_recv()
    def count(i, carry):
        target = lax.broadcasted_iota(jnp.int32, (own_rows, BLOCK), 0) + (group_base + cent * own_rows)
        for j in range(ids_all.shape[2] // BLOCK):
            carry = carry + jnp.where(target == ids_all[i, :, j * BLOCK:(j + 1) * BLOCK], 1.0, 0.0)
        return carry

    counts = lax.fori_loop(0, ids_all.shape[0], count, jnp.zeros((own_rows, BLOCK), F32))
    counts = jnp.maximum(jnp.sum(counts, axis=1, keepdims=True), 1.0)

    inverse = 1.0 / counts
    fetches[3].wait()
    squares = jnp.zeros((own_rows, 1), F32)
    for g in range(4):
        sums[g].wait()
        values = (part[g, 0] + part_q[g, 0] + part_q[g, 1]) * inverse + prev[:, columns(g)]
        c1_ref[:, columns(g)] = values
        squares = squares + jnp.sum(values * values, axis=1, keepdims=True)
    scale = lax.rsqrt(squares / pts.shape[1] + EPSILON)

    his, los = [], []
    for h in range(2):
        values = c1_ref[:, h * wide:(h + 1) * wide] * scale
        c1_ref[:, h * wide:(h + 1) * wide] = values
        hi = values.astype(BF16)
        his.append(hi)
        los.append((values - hi.astype(F32)).astype(BF16))

    def upper(h, d):
        pick = picks[h, d]
        sums = jnp.dot(pick, his[h], preferred_element_type=F32) + jnp.dot(
            pick, los[h], preferred_element_type=F32
        )
        up[h, d] = sums.reshape(RING, sub, wide)

    def scatter_up(h, step):
        j = ring(me[h][1], step)
        return Scatter(lambda d: up.at[h, d, j], up_f.at[h, step], up_q.at[h, step], lines[h][1])

    def settle(h, step):
        ups[h][step].wait()
        j = ring(me[h][1], step)
        low[h, j] = up[h, 0, j] + up_q[h, step, 0] + up_q[h, step, 1]

    ups = [[scatter_up(h, step) for step in range(RING)] for h in range(2)]
    lows = [
        Scatter(lambda d, h=h: low.at[h, ring(me[h][1], d)], low_f.at[h], low_q.at[h], lines[h][0]) for h in range(2)
    ]
    for h in range(2):
        upper(h, 2)
        for step in (2, 1, 3, 0):
            ups[h][step].far()
    for h in range(2):
        upper(h, 1)
        upper(h, 3)
        ups[h][2].near()
    for h in range(2):
        upper(h, 0)
    for h in range(2):
        ups[h][2].forward()
    for h in range(2):
        for step in (1, 3):
            ups[h][step].near()
    for h in range(2):
        for step in (1, 3):
            ups[h][step].forward()
    for h in range(2):
        ups[h][0].near()
        ups[h][0].forward()
    for h in range(2):
        settle(h, 2)
        lows[h].far()
    for h in range(2):
        settle(h, 1)
        settle(h, 3)
        lows[h].near()
    for h in range(2):
        lows[h].forward()
    tab["q1"].wait_recv()
    score(ring(x, 1) * 2 + other)
    for h in range(2):
        settle(h, 0)
    squares = jnp.zeros((sub, 1), F32)
    values = []
    for h in range(2):
        lows[h].wait()
        values.append(low[h, me[h][1]] + low_q[h, 0] + low_q[h, 1])
        squares = squares + jnp.sum(values[h] * values[h], axis=1, keepdims=True)
    scale = lax.rsqrt(squares / pts.shape[1] + EPSILON)
    for h in range(2):
        c2_ref[z, y, :, h * wide:(h + 1) * wide] = values[h] * scale

    def piece(h, i, j, rows=pl.ds(0, sub)):
        at = (i, j) if h == 0 else (j, i)
        return c2_ref.at[at[0], at[1], rows, pl.ds(h * wide, wide)]

    upper_half, lower_half = pl.ds(0, sub // 2), pl.ds(sub // 2, sub // 2)

    def spread(h, i, j, line):
        src = piece(h, i, j)
        return send(src, src, line(1)), send(src, src, line(-1))

    def spread_halves(h, i, j, line):
        high, low_rows = piece(h, i, j, upper_half), piece(h, i, j, lower_half)
        first_pair = send(high, high, line(1)), send(low_rows, low_rows, line(-1))
        return first_pair + (send(low_rows, low_rows, line(1)), send(high, high, line(-1)))

    def pass_on(pair, low_src, high_src, line):
        pair[0].wait_recv()
        first_copy = send(low_src, low_src, line(1))
        pair[1].wait_recv()
        return first_copy, send(high_src, high_src, line(-1))

    def pass_far(h, j, pair):
        i = me[h][0]
        return pass_on(
            pair, piece(h, ring(i, -1), j, upper_half), piece(h, ring(i, 1), j, lower_half), lines[h][1]
        )

    near_pairs, far_pairs, passed = [], [], []
    for h in range(2):
        i, j = me[h]
        near_pairs.append(spread_halves(h, i, j, lines[h][0]))
    for h in range(2):
        i, j = me[h]
        far_pairs.append({0: spread(h, i, j, lines[h][1])})
    score(ring(x, 2) * 2 + core)
    crossed = []
    for h in range(2):
        i, j = me[h]
        crossed.append(pass_on(
            near_pairs[h], piece(h, i, ring(j, -1), upper_half), piece(h, i, ring(j, 1), lower_half), lines[h][0]
        ))
    for h in range(2):
        i, j = me[h]
        near_pairs[h][2].wait_recv()
        far_pairs[h][-1] = spread(h, i, ring(j, -1), lines[h][1])
        near_pairs[h][3].wait_recv()
        far_pairs[h][1] = spread(h, i, ring(j, 1), lines[h][1])
    for h in range(2):
        passed.append(pass_far(h, me[h][1], far_pairs[h][0]))
    tab["q2"].wait_recv()
    score(ring(x, 2) * 2 + other)
    for h in range(2):
        i, j = me[h]
        for copy in crossed[h]:
            copy.wait_recv()
        far_pairs[h][2] = spread_halves(h, i, ring(j, 2), lines[h][1])
    for step in (-1, 1, 2):
        for h in range(2):
            passed.append(pass_far(h, ring(me[h][1], step), far_pairs[h][step]))
    for h in range(2):
        passed.append(far_pairs[h][2][2:])
    totals = jnp.sum(score_acc[...], axis=0, keepdims=True)
    for b in range(pts.shape[0] // BLOCK):
        score_ref[b:b + 1, :] = jnp.log(totals[:, b * BLOCK:(b + 1) * BLOCK])
    for pair in passed:
        for copy in pair:
            copy.wait_recv()
    for copy in copies:
        copy.wait_send()
    assert len(copies) == N_COPIES


N_COPIES = 167
N_PIECES = 4


def put_out(*refs):
    sources, targets, sem = refs[:3], refs[3:6], refs[6]
    moves = []
    for k, (source, target) in enumerate(zip(sources, targets)):
        pieces = N_PIECES if k < 2 else 1
        step = source.shape[0] // pieces
        for i in range(pieces):
            rows = pl.ds(i * step, step)
            moves.append(pltpu.make_async_copy(source.at[rows], target.at[rows], sem.at[k, i]))
    for move in moves:
        move.start()
    for move in moves:
        move.wait()


def shards(points, point_cluster, cand_blocks, cent1_prev, parent, cent2_prev):
    rows, width = points.shape
    wide = width // 2
    owned = cent1_prev.shape[0]
    table_rows = cent2_prev.shape[0]
    n_dp = lax.axis_size("dp")
    n_cent = lax.axis_size("cent")
    block = table_rows // RING
    sub = block // RING
    hbm = pl.BlockSpec(memory_space=pltpu.HBM)
    vmem = pl.BlockSpec(memory_space=pltpu.VMEM)
    cent1_new, cent2_new, score = pl.pallas_call(
        kernel,
        out_shape=(
            jax.ShapeDtypeStruct((owned, width), F32),
            jax.ShapeDtypeStruct((RING, RING, sub, width), F32),
            jax.ShapeDtypeStruct((rows // BLOCK, BLOCK), F32),
        ),
        in_specs=[hbm] * 6,
        out_specs=(vmem, vmem, vmem),
        scratch_shapes=[
            pltpu.VMEM((rows, width), BF16),
            pltpu.VMEM((rows, width), BF16),
            pltpu.VMEM((2, 3, rows, wide), BF16),
            pltpu.VMEM((table_rows, width), BF16),
            pltpu.VMEM((n_dp, table_rows, width), BF16),
            pltpu.VMEM((n_dp, table_rows // BLOCK, rows), F32),
            pltpu.VMEM((table_rows // BLOCK, rows), F32),
            pltpu.VMEM((n_cent, 1, rows), jnp.int32),
            pltpu.VMEM((RING * owned, rows // 2), BF16),
            pltpu.VMEM((2, RING, owned, rows), BF16),
            pltpu.VMEM((2, RING, block, owned), BF16),
            pltpu.VMEM((4, RING, owned, wide // 2), F32),
            pltpu.VMEM((4, 2, owned // 2, wide // 2), F32),
            pltpu.VMEM((4, 2, owned, wide // 2), F32),
            pltpu.VMEM((owned, width), F32),
            pltpu.VMEM((2, RING, RING, sub, wide), F32),
            pltpu.VMEM((2, RING, 2, sub // 2, wide), F32),
            pltpu.VMEM((2, RING, 2, sub, wide), F32),
            pltpu.VMEM((2, RING, sub, wide), F32),
            pltpu.VMEM((2, 2, sub // 2, wide), F32),
            pltpu.VMEM((2, 2, sub, wide), F32),
            pltpu.VMEM((3, 1, rows), jnp.int32),
            pltpu.SMEM(cand_blocks.shape, jnp.int32),
            pltpu.VMEM((1, owned), jnp.int32),
            pltpu.SemaphoreType.DMA((N_COPIES,)),
            pltpu.SemaphoreType.DMA((N_COPIES,)),
            pltpu.SemaphoreType.DMA((6,)),
        ],
        compiler_params=pltpu.CompilerParams(
            collective_id=0, has_side_effects=True, vmem_limit_bytes=44 * 1024 * 1024
        ),
    )(
        pltpu.with_memory_space_constraint(points, pltpu.HBM),
        pltpu.with_memory_space_constraint(point_cluster.reshape(1, rows), pltpu.HBM),
        pltpu.with_memory_space_constraint(cand_blocks, pltpu.HBM),
        pltpu.with_memory_space_constraint(cent1_prev, pltpu.HBM),
        pltpu.with_memory_space_constraint(parent.reshape(1, owned), pltpu.HBM),
        pltpu.with_memory_space_constraint(cent2_prev, pltpu.HBM),
    )
    results = (cent1_new, cent2_new, score)
    cent1_new, cent2_new, score = pl.pallas_call(
        put_out,
        out_shape=tuple(jax.ShapeDtypeStruct(r.shape, r.dtype) for r in results),
        in_specs=[vmem] * 3,
        out_specs=(hbm,) * 3,
        scratch_shapes=[pltpu.SemaphoreType.DMA((3, N_PIECES))],
        compiler_params=pltpu.CompilerParams(vmem_limit_bytes=16 * 1024 * 1024),
    )(*results)
    return cent1_new, cent2_new.reshape(table_rows, width), score.reshape(rows)


def solution(mesh):
    placed = (
        P(("dp", "cent"), None),
        P(("dp", "cent")),
        P(("dp", "cent"), None),
        P(("dp", "cent"), None),
        P(("dp", "cent")),
        P("dp", None),
    )
    return jax.shard_map(
        shards,
        mesh=mesh,
        in_specs=placed,
        out_specs=(P(("dp", "cent"), None), P("dp", None), P(("dp", "cent"))),
        check_vma=False,
    )
```

```python
import jax
import jax.numpy as jnp
from jax import lax
from jax.experimental import pallas as pl
from jax.experimental.pallas import tpu as pltpu
from jax.sharding import PartitionSpec as P

BLOCK = 128
EPSILON = 1e-06
SHARPNESS = 20.0
RING = 4
MESH = pl.DeviceIdType.MESH
F32 = jnp.float32
BF16 = jnp.bfloat16


def rms_norm(values):
    return values * lax.rsqrt(jnp.mean(values * values, axis=-1, keepdims=True) + EPSILON)


def kernel(
    pts_hbm, ids_hbm, cand_hbm, prev_hbm, parent_hbm, tab_hbm,
    c1_ref, c2_ref, score_ref,
    pts, units, gathered, raw, table, mask, score_acc, ids_all, onehot, across_hot, picks, part, part_f, part_q, prev,
    up, up_f, up_q, low, low_f, low_q, column_ids, cand_ref, parent_ref, send_sem, recv_sem, local_sem,
):
    dp = lax.axis_index("dp")
    cent = lax.axis_index("cent")
    x, core = dp // 2, lax.rem(dp, 2)
    z, y = cent // RING, lax.rem(cent, RING)

    def ring(at, step):
        return lax.rem(at + step + RING, RING)

    def y_at(step):
        return {"cent": z * RING + ring(y, step)}

    def z_at(step):
        return {"cent": ring(z, step) * RING + y}

    def x_at(step):
        return {"dp": ring(x, step) * 2 + core}

    partner = {"dp": x * 2 + 1 - core}
    copies = []

    def send(src, dst, device):
        at = len(copies)
        copy = pltpu.make_async_remote_copy(
            src_ref=src, dst_ref=dst, send_sem=send_sem.at[at], recv_sem=recv_sem.at[at],
            device_id=device, device_id_type=MESH,
        )
        copy.start()
        copies.append(copy)
        return copy

    fetches = [
        pltpu.make_async_copy(tab_hbm, raw, local_sem.at[0]),
        pltpu.make_async_copy(pts_hbm, pts, local_sem.at[1]),
        pltpu.make_async_copy(ids_hbm, ids_all.at[cent], local_sem.at[2]),
        pltpu.make_async_copy(prev_hbm, prev, local_sem.at[3]),
        pltpu.make_async_copy(cand_hbm, cand_ref, local_sem.at[4]),
        pltpu.make_async_copy(parent_hbm, parent_ref, local_sem.at[5]),
    ]
    for fetch in fetches:
        fetch.start()

    barrier = pltpu.get_barrier_semaphore()
    peers = [y_at(1), y_at(-1), z_at(1), z_at(-1), x_at(1), x_at(-1), partner]
    for peer in peers:
        pl.semaphore_signal(barrier, inc=1, device_id=peer, device_id_type=MESH)
    pl.semaphore_wait(barrier, len(peers))

    half = pts.shape[0] // 2
    wide = pts.shape[1] // 2
    part_w = wide // 2
    lines = ((y_at, z_at), (z_at, y_at))

    row_near = [send(ids_hbm, ids_all.at[cent], y_at(1)), send(ids_hbm, ids_all.at[cent], y_at(-1))]
    column_near = [send(ids_hbm, column_ids.at[0], z_at(1)), send(ids_hbm, column_ids.at[1], z_at(-1))]

    first, last = pl.ds(0, half), pl.ds(half, half)
    moved = []
    for h in range(2):
        cols = pl.ds(h * wide, wide)
        near = lines[h][0]
        moved.append(dict(
            pa=send(pts_hbm.at[first, cols], gathered.at[h, 0, first], near(1)),
            mb=send(pts_hbm.at[last, cols], gathered.at[h, 1, last], near(-1)),
        ))
    rows_t = raw.shape[0]
    top, bottom = pl.ds(0, rows_t // 2), pl.ds(rows_t // 2, rows_t // 2)
    fetches[0].wait()

    def norm_table(i, carry):
        rows = pl.ds(pl.multiple_of(i * 64, 64), 64)
        table[dp, rows] = rms_norm(raw[rows].astype(F32)).astype(BF16)
        return carry

    lax.fori_loop(0, rows_t // 64, norm_table, 0)
    own = table.at[dp]
    tab = dict(
        pa=send(own.at[top], own.at[top], x_at(1)),
        mb=send(own.at[bottom], own.at[bottom], x_at(-1)),
        cp=send(own, own, partner),
    )

    for copy in row_near + column_near:
        copy.wait_recv()
    passed_ids = ids_all.at[z * RING + ring(y, -1)]
    row_far = send(passed_ids, passed_ids, y_at(1))
    column_far = send(column_ids.at[0], column_ids.at[2], z_at(1))

    for h in range(2):
        cols = pl.ds(h * wide, wide)
        near = lines[h][0]
        moved[h].update(
            pb=send(pts_hbm.at[last, cols], gathered.at[h, 0, last], near(1)),
            ma=send(pts_hbm.at[first, cols], gathered.at[h, 1, first], near(-1)),
        )
    tab.update(
        pb=send(own.at[bottom], own.at[bottom], x_at(1)),
        ma=send(own.at[top], own.at[top], x_at(-1)),
    )

    fetches[4].wait()
    fetches[5].wait()
    for b in range(pts.shape[0] // BLOCK):
        rows = lax.broadcasted_iota(jnp.int32, (mask.shape[0], mask.shape[1], BLOCK), 0) * mask.shape[1]
        rows = rows + lax.broadcasted_iota(jnp.int32, (mask.shape[0], mask.shape[1], BLOCK), 1)
        hit = jnp.zeros(rows.shape, F32)
        for j in range(cand_ref.shape[1]):
            hit = jnp.where(rows == cand_ref[b, j], 1.0, hit)
        mask[:, :, b * BLOCK:(b + 1) * BLOCK] = hit
    score_acc[...] = jnp.zeros_like(score_acc)

    fetches[1].wait()

    def norm_points(i, carry):
        rows = pl.ds(pl.multiple_of(i * 64, 64), 64)
        units[rows] = rms_norm(pts[rows].astype(F32)).astype(BF16)
        return carry

    lax.fori_loop(0, pts.shape[0] // 64, norm_points, 0)

    def score(slot):
        def step(i, carry):
            at = pl.ds(pl.multiple_of(i * 256, 256), 256)
            dots = lax.dot_general(
                table[slot], units[at], (((1,), (1,)), ((), ())), preferred_element_type=F32
            )
            weights = jnp.exp(dots * (SHARPNESS / pts.shape[1]))
            sums = jnp.sum(weights.reshape(mask.shape[1], BLOCK, 256), axis=1)
            score_acc[:, at] += sums * mask[slot, :, at]
            return carry

        lax.fori_loop(0, pts.shape[0] // 256, step, 0)

    own_rows = part.shape[2]
    group_base = dp * (RING * RING * own_rows)

    def owner_base(h, d):
        at = (ring(z, d) * RING + y) if h == 0 else (z * RING + ring(y, d))
        return group_base + at * own_rows

    def ids_of(h, step):
        if h == 0 or step == 0:
            return ids_all.at[z * RING + ring(y, step)]
        return column_ids.at[{-1: 0, 1: 1, 2: 2}[step]]

    def accumulate(h, step, points, lo, fresh=False):
        ids = ids_of(h, step)[:, lo:lo + half]
        for d in range(RING):
            target = lax.broadcasted_iota(jnp.int32, (own_rows, half), 0) + owner_base(h, d)
            onehot[d * own_rows:(d + 1) * own_rows] = jnp.where(target == ids, 1.0, 0.0).astype(BF16)
        sums = jnp.dot(onehot[...], points, preferred_element_type=F32)
        for d in range(RING):
            for k in range(2):
                piece = sums[d * own_rows:(d + 1) * own_rows, k * part_w:(k + 1) * part_w]
                if fresh:
                    part[2 * k + h, d] = piece
                else:
                    part[2 * k + h, d] += piece

    def prepare(h):
        ids = ids_of(h, 2)[...]
        for d in range(RING):
            target = lax.broadcasted_iota(jnp.int32, (own_rows, 2 * half), 0) + owner_base(h, d)
            across_hot[h, d] = jnp.where(target == ids, 1.0, 0.0).astype(BF16)

    def finish(h, k, d):
        part[2 * k + h, d] += jnp.dot(
            across_hot[h, d], gathered[h, 2, :, k * part_w:(k + 1) * part_w], preferred_element_type=F32
        )

    fetches[2].wait()
    for h in range(2):
        cols = slice(h * wide, (h + 1) * wide)
        accumulate(h, 0, pts[0:half, cols], 0, fresh=True)
        accumulate(h, 0, pts[half:, cols], half)
    score(dp)

    def pass_points(h, k):
        near = lines[h][0]
        cols = pl.ds(k * part_w, part_w)
        moved[h]["fa", k] = send(gathered.at[h, 0, first, cols], gathered.at[h, 2, first, cols], near(1))
        moved[h]["fb", k] = send(gathered.at[h, 1, last, cols], gathered.at[h, 2, last, cols], near(-1))

    row_far.wait_recv()
    rows_ids = ids_all.at[pl.ds(z * RING, RING)]
    rows_near = [send(rows_ids, rows_ids, z_at(1)), send(rows_ids, rows_ids, z_at(-1))]
    for h in range(2):
        moved[h]["pa"].wait_recv()
        moved[h]["mb"].wait_recv()
        for k in range(2):
            pass_points(h, k)
    before = table.at[ring(x, -1) * 2 + core]
    after = table.at[ring(x, 1) * 2 + core]
    across = table.at[ring(x, 2) * 2 + core]
    tab["pa"].wait_recv()
    tab["fa"] = send(before.at[top], before.at[top], x_at(1))
    tab["mb"].wait_recv()
    tab["fb"] = send(after.at[bottom], after.at[bottom], x_at(-1))
    column_far.wait_recv()
    for h in range(2):
        accumulate(h, -1, gathered[h, 0, 0:half], 0)
        accumulate(h, 1, gathered[h, 1, half:], half)

    tab["cp"].wait_recv()
    other = 1 - core
    score(x * 2 + other)
    sub = up.shape[3]
    block = sub * RING
    local = parent_ref[...] - dp * (RING * block)
    swapped = (
        lax.shift_right_logical(local & (block - 1), 5) * block
        + lax.shift_right_logical(local, 7) * sub
        + (local & (sub - 1))
    )
    places = (local, swapped)
    me = ((z, y), (y, z))
    for h in range(2):
        prepare(h)
        for d in range(RING):
            target = lax.broadcasted_iota(jnp.int32, (block, own_rows), 0) + ring(me[h][0], d) * block
            picks[h, d] = jnp.where(target == places[h], 1.0, 0.0).astype(BF16)

    for h in range(2):
        moved[h]["pb"].wait_recv()
        accumulate(h, -1, gathered[h, 0, half:], half)
        moved[h]["ma"].wait_recv()
        accumulate(h, 1, gathered[h, 1, 0:half], 0)
    tab["pb"].wait_recv()
    tab["q0"] = send(before, before, partner)
    tab["ma"].wait_recv()
    tab["q1"] = send(after, after, partner)

    for copy in rows_near:
        copy.wait_recv()
    passed_ids = ids_all.at[pl.ds(ring(z, -1) * RING, RING)]
    rows_far = send(passed_ids, passed_ids, z_at(1))

    class Scatter:
        def __init__(self, src, f, q, line):
            self.src, self.f, self.q, self.line = src, f, q, line
            self.n = q.shape[1] // 2

        def far(self):
            a, b = pl.ds(0, self.n), pl.ds(self.n, self.n)
            self.c2a = send(self.src(2).at[a], self.f.at[0], self.line(1))
            self.c2b = send(self.src(2).at[b], self.f.at[1], self.line(-1))

        def near(self):
            a, b = pl.ds(0, self.n), pl.ds(self.n, self.n)
            self.c1b = send(self.src(1).at[b], self.q.at[0, b], self.line(1))
            self.c3a = send(self.src(3).at[a], self.q.at[1, a], self.line(-1))

        def forward(self):
            a, b = pl.ds(0, self.n), pl.ds(self.n, self.n)
            self.c2a.wait_recv()
            self.src(1)[a] += self.f[0]
            self.c1a = send(self.src(1).at[a], self.q.at[0, a], self.line(1))
            self.c2b.wait_recv()
            self.src(3)[b] += self.f[1]
            self.c3b = send(self.src(3).at[b], self.q.at[1, b], self.line(-1))

        def wait(self):
            for copy in (self.c1b, self.c3a, self.c1a, self.c3b):
                copy.wait_recv()

    def scatter(src, f, q, stage):
        return [Scatter(lambda d, g=g: src(g, d), f.at[g], q.at[g], lines[g % 2][stage]) for g in range(4)]

    def columns(g):
        at = (g % 2) * wide + (g // 2) * part_w
        return slice(at, at + part_w)

    sums = scatter(lambda g, d: part.at[g, d], part_f, part_q, 1)
    for k in range(2):
        for h in range(2):
            moved[h]["fa", k].wait_recv()
            moved[h]["fb", k].wait_recv()
            finish(h, k, 2)
            sums[2 * k + h].far()
        for h in range(2):
            finish(h, k, 1)
            finish(h, k, 3)
            sums[2 * k + h].near()
        for h in range(2):
            finish(h, k, 0)
        score(ring(x, -1 + 2 * k) * 2 + core)
    sums[0].forward()
    sums[1].forward()
    tab["fa"].wait_recv()
    tab["fb"].wait_recv()
    tab["q2"] = send(across, across, partner)
    sums[2].forward()
    sums[3].forward()
    tab["q0"].wait_recv()
    score(ring(x, -1) * 2 + other)
    rows_far.wait_recv()
    def count(i, carry):
        target = lax.broadcasted_iota(jnp.int32, (own_rows, BLOCK), 0) + (group_base + cent * own_rows)
        for j in range(ids_all.shape[2] // BLOCK):
            carry = carry + jnp.where(target == ids_all[i, :, j * BLOCK:(j + 1) * BLOCK], 1.0, 0.0)
        return carry

    counts = lax.fori_loop(0, ids_all.shape[0], count, jnp.zeros((own_rows, BLOCK), F32))
    counts = jnp.maximum(jnp.sum(counts, axis=1, keepdims=True), 1.0)

    inverse = 1.0 / counts
    fetches[3].wait()
    squares = jnp.zeros((own_rows, 1), F32)
    for g in range(4):
        sums[g].wait()
        values = (part[g, 0] + part_q[g, 0] + part_q[g, 1]) * inverse + prev[:, columns(g)]
        c1_ref[:, columns(g)] = values
        squares = squares + jnp.sum(values * values, axis=1, keepdims=True)
    scale = lax.rsqrt(squares / pts.shape[1] + EPSILON)

    his, los = [], []

    def upper(h, d):
        pick = picks[h, d]
        sums = jnp.dot(pick, his[h], preferred_element_type=F32) + jnp.dot(
            pick, los[h], preferred_element_type=F32
        )
        up[h, d] = sums.reshape(RING, sub, wide)

    def scatter_up(h, step):
        j = ring(me[h][1], step)
        return Scatter(lambda d: up.at[h, d, j], up_f.at[h, step], up_q.at[h, step], lines[h][1])

    def settle(h, step):
        ups[h][step].wait()
        j = ring(me[h][1], step)
        low[h, j] = up[h, 0, j] + up_q[h, step, 0] + up_q[h, step, 1]

    ups = [[scatter_up(h, step) for step in range(RING)] for h in range(2)]
    lows = [
        Scatter(lambda d, h=h: low.at[h, ring(me[h][1], d)], low_f.at[h], low_q.at[h], lines[h][0]) for h in range(2)
    ]
    for h in range(2):
        values = c1_ref[:, h * wide:(h + 1) * wide] * scale
        c1_ref[:, h * wide:(h + 1) * wide] = values
        hi = values.astype(BF16)
        his.append(hi)
        los.append((values - hi.astype(F32)).astype(BF16))
        upper(h, 2)
        for step in (2, 1, 3, 0):
            ups[h][step].far()
    for h in range(2):
        upper(h, 1)
        upper(h, 3)
        ups[h][2].near()
    for h in range(2):
        upper(h, 0)
    for h in range(2):
        ups[h][2].forward()
    for h in range(2):
        for step in (1, 3):
            ups[h][step].near()
    for h in range(2):
        for step in (1, 3):
            ups[h][step].forward()
    for h in range(2):
        ups[h][0].near()
        ups[h][0].forward()
    for h in range(2):
        settle(h, 2)
        lows[h].far()
    for h in range(2):
        settle(h, 1)
        settle(h, 3)
        lows[h].near()
    for h in range(2):
        lows[h].forward()
    tab["q1"].wait_recv()
    score(ring(x, 1) * 2 + other)
    for h in range(2):
        settle(h, 0)
    squares = jnp.zeros((sub, 1), F32)
    values = []
    for h in range(2):
        lows[h].wait()
        values.append(low[h, me[h][1]] + low_q[h, 0] + low_q[h, 1])
        squares = squares + jnp.sum(values[h] * values[h], axis=1, keepdims=True)
    scale = lax.rsqrt(squares / pts.shape[1] + EPSILON)
    for h in range(2):
        c2_ref[z, y, :, h * wide:(h + 1) * wide] = values[h] * scale

    def piece(h, i, j, rows=pl.ds(0, sub)):
        at = (i, j) if h == 0 else (j, i)
        return c2_ref.at[at[0], at[1], rows, pl.ds(h * wide, wide)]

    upper_half, lower_half = pl.ds(0, sub // 2), pl.ds(sub // 2, sub // 2)

    def spread(h, i, j, line):
        src = piece(h, i, j)
        return send(src, src, line(1)), send(src, src, line(-1))

    def spread_halves(h, i, j, line):
        high, low_rows = piece(h, i, j, upper_half), piece(h, i, j, lower_half)
        first_pair = send(high, high, line(1)), send(low_rows, low_rows, line(-1))
        return first_pair + (send(low_rows, low_rows, line(1)), send(high, high, line(-1)))

    def pass_on(pair, low_src, high_src, line):
        pair[0].wait_recv()
        first_copy = send(low_src, low_src, line(1))
        pair[1].wait_recv()
        return first_copy, send(high_src, high_src, line(-1))

    def pass_far(h, j, pair):
        i = me[h][0]
        return pass_on(
            pair, piece(h, ring(i, -1), j, upper_half), piece(h, ring(i, 1), j, lower_half), lines[h][1]
        )

    near_pairs, far_pairs, passed = [], [], []
    for h in range(2):
        i, j = me[h]
        near_pairs.append(spread_halves(h, i, j, lines[h][0]))
    for h in range(2):
        i, j = me[h]
        far_pairs.append({0: spread(h, i, j, lines[h][1])})
    score(ring(x, 2) * 2 + core)
    crossed = []
    for h in range(2):
        i, j = me[h]
        crossed.append(pass_on(
            near_pairs[h], piece(h, i, ring(j, -1), upper_half), piece(h, i, ring(j, 1), lower_half), lines[h][0]
        ))
    for h in range(2):
        i, j = me[h]
        near_pairs[h][2].wait_recv()
        far_pairs[h][-1] = spread(h, i, ring(j, -1), lines[h][1])
        near_pairs[h][3].wait_recv()
        far_pairs[h][1] = spread(h, i, ring(j, 1), lines[h][1])
    for h in range(2):
        passed.append(pass_far(h, me[h][1], far_pairs[h][0]))
    tab["q2"].wait_recv()
    score(ring(x, 2) * 2 + other)
    for h in range(2):
        i, j = me[h]
        for copy in crossed[h]:
            copy.wait_recv()
        far_pairs[h][2] = spread_halves(h, i, ring(j, 2), lines[h][1])
    for step in (-1, 1, 2):
        for h in range(2):
            passed.append(pass_far(h, ring(me[h][1], step), far_pairs[h][step]))
    for h in range(2):
        passed.append(far_pairs[h][2][2:])
    totals = jnp.sum(score_acc[...], axis=0, keepdims=True)
    for b in range(pts.shape[0] // BLOCK):
        score_ref[b:b + 1, :] = jnp.log(totals[:, b * BLOCK:(b + 1) * BLOCK])
    for pair in passed:
        for copy in pair:
            copy.wait_recv()
    for copy in copies:
        copy.wait_send()
    assert len(copies) == N_COPIES


N_COPIES = 167
N_PIECES = 4


def put_out(*refs):
    sources, targets, sem = refs[:3], refs[3:6], refs[6]
    moves = []
    for k, (source, target) in enumerate(zip(sources, targets)):
        pieces = N_PIECES if k < 2 else 1
        step = source.shape[0] // pieces
        for i in range(pieces):
            rows = pl.ds(i * step, step)
            moves.append(pltpu.make_async_copy(source.at[rows], target.at[rows], sem.at[k, i]))
    for move in moves:
        move.start()
    for move in moves:
        move.wait()


def shards(points, point_cluster, cand_blocks, cent1_prev, parent, cent2_prev):
    rows, width = points.shape
    wide = width // 2
    owned = cent1_prev.shape[0]
    table_rows = cent2_prev.shape[0]
    n_dp = lax.axis_size("dp")
    n_cent = lax.axis_size("cent")
    block = table_rows // RING
    sub = block // RING
    hbm = pl.BlockSpec(memory_space=pltpu.HBM)
    vmem = pl.BlockSpec(memory_space=pltpu.VMEM)
    cent1_new, cent2_new, score = pl.pallas_call(
        kernel,
        out_shape=(
            jax.ShapeDtypeStruct((owned, width), F32),
            jax.ShapeDtypeStruct((RING, RING, sub, width), F32),
            jax.ShapeDtypeStruct((rows // BLOCK, BLOCK), F32),
        ),
        in_specs=[hbm] * 6,
        out_specs=(vmem, vmem, vmem),
        scratch_shapes=[
            pltpu.VMEM((rows, width), BF16),
            pltpu.VMEM((rows, width), BF16),
            pltpu.VMEM((2, 3, rows, wide), BF16),
            pltpu.VMEM((table_rows, width), BF16),
            pltpu.VMEM((n_dp, table_rows, width), BF16),
            pltpu.VMEM((n_dp, table_rows // BLOCK, rows), F32),
            pltpu.VMEM((table_rows // BLOCK, rows), F32),
            pltpu.VMEM((n_cent, 1, rows), jnp.int32),
            pltpu.VMEM((RING * owned, rows // 2), BF16),
            pltpu.VMEM((2, RING, owned, rows), BF16),
            pltpu.VMEM((2, RING, block, owned), BF16),
            pltpu.VMEM((4, RING, owned, wide // 2), F32),
            pltpu.VMEM((4, 2, owned // 2, wide // 2), F32),
            pltpu.VMEM((4, 2, owned, wide // 2), F32),
            pltpu.VMEM((owned, width), F32),
            pltpu.VMEM((2, RING, RING, sub, wide), F32),
            pltpu.VMEM((2, RING, 2, sub // 2, wide), F32),
            pltpu.VMEM((2, RING, 2, sub, wide), F32),
            pltpu.VMEM((2, RING, sub, wide), F32),
            pltpu.VMEM((2, 2, sub // 2, wide), F32),
            pltpu.VMEM((2, 2, sub, wide), F32),
            pltpu.VMEM((3, 1, rows), jnp.int32),
            pltpu.SMEM(cand_blocks.shape, jnp.int32),
            pltpu.VMEM((1, owned), jnp.int32),
            pltpu.SemaphoreType.DMA((N_COPIES,)),
            pltpu.SemaphoreType.DMA((N_COPIES,)),
            pltpu.SemaphoreType.DMA((6,)),
        ],
        compiler_params=pltpu.CompilerParams(
            collective_id=0, has_side_effects=True, vmem_limit_bytes=44 * 1024 * 1024
        ),
    )(
        pltpu.with_memory_space_constraint(points, pltpu.HBM),
        pltpu.with_memory_space_constraint(point_cluster.reshape(1, rows), pltpu.HBM),
        pltpu.with_memory_space_constraint(cand_blocks, pltpu.HBM),
        pltpu.with_memory_space_constraint(cent1_prev, pltpu.HBM),
        pltpu.with_memory_space_constraint(parent.reshape(1, owned), pltpu.HBM),
        pltpu.with_memory_space_constraint(cent2_prev, pltpu.HBM),
    )
    results = (cent1_new, cent2_new, score)
    cent1_new, cent2_new, score = pl.pallas_call(
        put_out,
        out_shape=tuple(jax.ShapeDtypeStruct(r.shape, r.dtype) for r in results),
        in_specs=[vmem] * 3,
        out_specs=(hbm,) * 3,
        scratch_shapes=[pltpu.SemaphoreType.DMA((3, N_PIECES))],
        compiler_params=pltpu.CompilerParams(vmem_limit_bytes=16 * 1024 * 1024),
    )(*results)
    return cent1_new, cent2_new.reshape(table_rows, width), score.reshape(rows)


def solution(mesh):
    placed = (
        P(("dp", "cent"), None),
        P(("dp", "cent")),
        P(("dp", "cent"), None),
        P(("dp", "cent"), None),
        P(("dp", "cent")),
        P("dp", None),
    )
    return jax.shard_map(
        shards,
        mesh=mesh,
        in_specs=placed,
        out_specs=(P(("dp", "cent"), None), P("dp", None), P(("dp", "cent"))),
        check_vma=False,
    )
```
